512 devices in a mesh: tm: 8 (over x, core), row: 64 (over z, y).
Axes of the slice: x: 4, y: 8, z: 8, core: 2. Of those that a mesh axis runs over, the one named last changes fastest.
Arguments:
- snapshots: float32 [65536, 1024], P('row', 'tm'), may hold values from -6 to 6
- sketches: float32 [3, 256, 128], replicated, may hold values from -0.375 to 0.375
Outputs:
- coefficients: float32 [128, 1024], P(None, 'tm')
- deflated: float32 [65536, 1024], P('row', 'tm')
The draws below stay inside these ranges and needn't reach their ends.
All inputs are finite; a program needn't handle non-finite values.
Results may differ from the reference program's by a relative error of at most 0.00024.
Values sent between devices are 32-bit elements; how exact they have to be, the bound alone decides.
A program may use at most 64 MiB of HBM per device.

```python
import jax
import jax.numpy as jnp
from jax import lax

MODES = 128
NS_STEPS = 5
ROWS = 65536
SNAPS = 1024
LEVELS = 3
N_TM = 8


def level_of(stream_key, extent, shards, low, high):
    level = 1.0
    for axis_at, shards_of in shards:
        draws = jax.random.uniform(jax.random.fold_in(jax.random.fold_in(stream_key, 6), axis_at), (shards_of,), jnp.float32, low / len(shards), high / len(shards))
        level = level * jnp.repeat(jnp.exp(draws), extent[axis_at] // shards_of).reshape((-1,) + (1,) * (len(extent) - 1 - axis_at))
    return level


def noise(stream_key, dims, scale, bound, shards=(), kind=jnp.bfloat16):
    result = jax.random.normal(stream_key, dims, jnp.float32) * scale
    if len(shards) > 0:
        result = level_of(stream_key, dims, shards, -0.22, 0.18) * result
    return jnp.clip(result, min=-bound, max=bound).astype(kind)


def setup_inputs(seed: int = 0) -> dict:
    key_list = jax.random.split(jax.random.key(seed), 3)
    return {
        "snapshots": noise(key_list[0], (ROWS, SNAPS), 1.0, 6.0, ((0, 64), (1, 8)), jnp.float32),
        "sketches": noise(key_list[1], (LEVELS, 2 * MODES, MODES), (2 * MODES) ** -0.5, 0.375, (), jnp.float32),
    }


HIGH = lax.Precision.HIGHEST

def inverse_root(matrix):
    frob_scale = jnp.sqrt(jnp.sum(matrix * matrix) + 1e-06)
    ident = jnp.eye(matrix.shape[0], dtype=matrix.dtype)
    y_iter = matrix / frob_scale
    z_iter = ident
    for repeat in range(NS_STEPS):
        middle = 1.5 * ident - 0.5 * jnp.dot(z_iter, y_iter, precision=HIGH)
        y_iter = jnp.dot(y_iter, middle, precision=HIGH)
        z_iter = jnp.dot(middle, z_iter, precision=HIGH)
    return z_iter / jnp.sqrt(frob_scale)

def reference(snapshots, sketches):
    groups = snapshots.reshape(ROWS, N_TM, MODES).transpose(1, 0, 2)
    grams = jnp.einsum('nrk,nrj->nkj', groups, groups, precision=HIGH)
    roots = jax.vmap(inverse_root)(grams)
    mode_blocks = jnp.einsum('nrk,nkj->nrj', groups, roots, precision=HIGH)
    for tree_level in range(LEVELS):
        earlier = jnp.roll(mode_blocks, 2 ** tree_level, axis=0)
        joined = jnp.concatenate([earlier, mode_blocks], axis=2)
        sketch = sketches[tree_level]
        grams = jnp.einsum('nrk,nrj->nkj', joined, joined, precision=HIGH)
        reduced = jnp.einsum('nkj,jm->nkm', grams, sketch, precision=HIGH)
        temp_prod = jnp.einsum('nkj,njm->nkm', grams, reduced, precision=HIGH)
        small = jnp.einsum('nkm,nkp->nmp', reduced, temp_prod, precision=HIGH)
        roots = jax.vmap(inverse_root)(small)
        mixing = jnp.einsum('nkm,nmp->nkp', reduced, roots, precision=HIGH)
        mode_blocks = jnp.einsum('nrk,nkp->nrp', joined, mixing, precision=HIGH)
    coeff_blocks = jnp.einsum('nrk,nrj->nkj', mode_blocks, groups, precision=HIGH)
    removed = groups - jnp.einsum('nrk,nkj->nrj', mode_blocks, coeff_blocks, precision=HIGH)
    coefficients = coeff_blocks.transpose(1, 0, 2).reshape(MODES, SNAPS)
    deflated = removed.transpose(1, 0, 2).reshape(ROWS, SNAPS)
    return (coefficients, deflated)
```

```python
import functools

import jax
import jax.numpy as jnp
from jax import lax
from jax.experimental import pallas as pl
from jax.experimental.pallas import tpu as pltpu
from jax.sharding import PartitionSpec as P

BF, F32 = jnp.bfloat16, jnp.float32
MESH = pl.DeviceIdType.MESH
NX, NC, NY, NZ = 4, 2, 8, 8
N = 128
ROWS = 1024
HALF = ROWS // 2


def split(a):
    high = a.astype(BF)
    return high, (a - high.astype(F32)).astype(BF)


def mm(a, b):
    ah, al = split(a)
    bh, bl = split(b)
    left = jnp.concatenate([ah, ah, al], 1)
    right = jnp.concatenate([bh, bl, bh], 0)
    return jnp.dot(left, right, preferred_element_type=F32)


def identity():
    down = lax.broadcasted_iota(jnp.int32, (N, N), 0)
    across = lax.broadcasted_iota(jnp.int32, (N, N), 1)
    return jnp.where(down == across, 1.0, 0.0).astype(F32)


def inverse_roots(grams, want_image=True):
    one = identity()
    scales = [jnp.sqrt(jnp.sum(a * a, keepdims=True) + 1e-06) for a in grams]
    ts = [a / s for a, s in zip(grams, scales)]
    zs = ms = [1.5 * one - 0.5 * t for t in ts]
    ts = [mm(mm(t, m), m) for t, m in zip(ts, ms)]
    for step in range(1, 5):
        ms = [1.5 * one - 0.5 * t for t in ts]
        if step == 4 and not want_image:
            zs = [mm(z, m) for z, m in zip(zs, ms)]
        else:
            both = [mm(jnp.concatenate([t, z], 0), m) for t, z, m in zip(ts, zs, ms)]
            zs = [b[N:] for b in both]
            ts = [mm(b[:N], m) for b, m in zip(both, ms)]
    return [z / jnp.sqrt(s) for z, s in zip(zs, scales)], ts


def sketched(t_p, t_g, cross, sketch):
    top = jnp.concatenate([t_p, cross.T], 1)
    bottom = jnp.concatenate([cross, t_g], 1)
    gram = jnp.concatenate([top, bottom], 0)
    s = mm(gram, sketch)
    return s, mm(s.T, mm(gram, s))


def tree(root, image, block, own, sketch, x_of):
    r = [root(o) for o in range(8)]
    s0, a0, e0 = [], [], []
    for j in range(4):
        cross = mm(mm(r[2 * j], block(2 * j, 2 * j + 1)), r[2 * j + 1])
        s, a = sketched(image(2 * j + 1), image(2 * j), cross, sketch(0))
        s0.append(s)
        a0.append(a)
    for j in range(4):
        e0.append(jnp.concatenate([mm(r[2 * j + 1], s0[j][:N]), mm(r[2 * j], s0[j][N:])], 0))
    cross1 = []
    for j in range(0, 4, 2):
        upper = jnp.concatenate([block(2 * j + 1, 2 * j + 3), block(2 * j + 1, 2 * j + 2)], 1)
        lower = jnp.concatenate([block(2 * j, 2 * j + 3), block(2 * j, 2 * j + 2)], 1)
        cross1.append(mm(e0[j].T, mm(jnp.concatenate([upper, lower], 0), e0[j + 1])))
    r1, t1 = inverse_roots(a0)
    s1, a1, e1 = [], [], []
    for j in range(2):
        cross = mm(mm(r1[2 * j], cross1[j]), r1[2 * j + 1])
        s, a = sketched(t1[2 * j + 1], t1[2 * j], cross, sketch(1))
        s1.append(s)
        a1.append(a)
    for j in range(2):
        upper = mm(e0[2 * j + 1], mm(r1[2 * j + 1], s1[j][:N]))
        lower = mm(e0[2 * j], mm(r1[2 * j], s1[j][N:]))
        e1.append(jnp.concatenate([upper, lower], 0))
    wide = [jnp.concatenate([block(a, b) for b in (7, 6, 5, 4)], 1) for a in (3, 2, 1, 0)]
    cross2 = mm(e1[0].T, mm(jnp.concatenate(wide, 0), e1[1]))
    near = jnp.concatenate([block(0, 3), block(0, 2), block(0, 1), own], 1)
    far = jnp.concatenate([block(0, 7), block(0, 6), block(0, 5), block(0, 4)], 1)
    w_far, w_near = mm(far, e1[1]), mm(near, e1[0])
    r2, t2 = inverse_roots(a1)
    s2, a2 = sketched(t2[1], t2[0], mm(mm(r2[0], cross2), r2[1]), sketch(2))
    h = mm(jnp.concatenate([mm(w_far, r2[1]), mm(w_near, r2[0])], 1), s2)
    upper = mm(e1[1], mm(r2[1], s2[:N]))
    lower = mm(e1[0], mm(r2[0], s2[N:]))
    x_all = jnp.concatenate([x_of(o) for o in range(7, -1, -1)], 1)
    base = mm(x_all, jnp.concatenate([upper, lower], 0))
    r3 = inverse_roots([a2], False)[0][0]
    coefficients = mm(h, r3).T
    return coefficients, x_of(0) - mm(base, mm(r3, coefficients))


def place():
    tm, row = lax.axis_index("tm"), lax.axis_index("row")
    return tm // NC, tm % NC, row % NY, row // NY


def device(x, c, y, z):
    return (x * NC + c, z * NY + y)


def rows_of(index, count):
    return pl.ds(pl.multiple_of(index * count, count), count)


def exchange(x_ref, xall, kall, rt, own, part, rsy, rsz, zsrc, lrow, lsy, lsz, leaves,
             g_s, g_r, c_s, c_r, y_s, y_r, z_s, z_r, p1_s, p1_r, p2_s, p2_r, p3_s, p3_r, p4_s, p4_r,
             ly_s, ly_r, lz_s, lz_r, la_s, la_r, b1_s, b1_r, b2_s, b2_r, b4_s, b4_r):
    x, c, y, z = place()
    left, right, across = (x + 3) % NX, (x + 1) % NX, (x + 2) % NX
    peers_x = [device((x + k) % NX, c, y, z) for k in range(1, NX)]
    peers_y = [device(x, c, (y + k) % NY, z) for k in range(1, NY)]
    peers_z = [device(x, c, y, (z + k) % NZ) for k in range(1, NZ)]
    partner = device(x, 1 - c, y, z)

    barrier = pltpu.get_barrier_semaphore()
    everyone = peers_x + peers_y + peers_z + [partner]
    for peer in everyone:
        pl.semaphore_signal(barrier, inc=1, device_id=peer, device_id_type=MESH)
    pl.semaphore_wait(barrier, len(everyone))

    def send(src, dst, s, r, peer):
        copy = pltpu.make_async_remote_copy(
            src_ref=src, dst_ref=dst, send_sem=s, recv_sem=r, device_id=peer, device_id_type=MESH
        )
        copy.start()
        return copy

    pending = []
    first, last = pl.ds(0, HALF), pl.ds(HALF, HALF)
    to_right, to_left = device(right, c, y, z), device(left, c, y, z)
    hops = []
    for k, (half, peer) in enumerate([(first, to_right), (last, to_left), (last, to_right), (first, to_left)]):
        hops.append(send(x_ref.at[half], xall.at[x, c, half], g_s.at[k], g_r.at[k], peer))
    pending += hops
    whole = send(x_ref, xall.at[x, c], c_s.at[6], c_r.at[6], partner)
    pending.append(whole)
    mine = x_ref[...]
    xall[x, c] = mine

    mine_h, mine_l = split(mine)
    mine_t = mine.T
    turned_h, turned_l = split(mine_t)
    turned = jnp.concatenate([turned_h, turned_h, turned_l], 1)

    def gram_with(high, low):
        return jnp.dot(turned, jnp.concatenate([high, low, high], 0), preferred_element_type=F32)

    lrow[...] = gram_with(mine_h, mine_l).reshape(2, 64, N)
    copies = [
        send(lrow.at[:, rows_of((y + k) % NY, 8), :], lsy.at[k - 1], ly_s.at[k - 1], ly_r.at[k - 1], peers_y[k - 1])
        for k in range(1, NY)
    ]
    total = lrow[:, rows_of(y, 8), :]
    for k, copy in enumerate(copies):
        copy.wait_recv()
        total += lsy[k]
    pending += copies
    lsz[NZ - 1] = total
    copies = [
        send(lsz.at[NZ - 1], lsz.at[k - 1], lz_s.at[k - 1], lz_r.at[k - 1], peers_z[k - 1])
        for k in range(1, NZ)
    ]

    def passed(k, source, half):
        return send(xall.at[source, c, half], xall.at[source, c, half], c_s.at[k], c_r.at[k], partner)

    hops[0].wait_recv()
    hops.append(send(xall.at[left, c, first], xall.at[left, c, first], g_s.at[4], g_r.at[4], to_right))
    hops[1].wait_recv()
    hops.append(send(xall.at[right, c, last], xall.at[right, c, last], g_s.at[5], g_r.at[5], to_left))
    on_chip = [passed(0, left, first), passed(1, right, last)]

    for copy in copies:
        copy.wait_recv()
    pending += copies
    total = jnp.zeros((2, 8, N), F32)
    for source in range(NZ):
        total += lsz[(z - source + NZ - 1) % NZ]
    own[:, rows_of(y, 8), :] = total
    copies = [
        send(own.at[:, rows_of(y, 8), :], own.at[:, rows_of(y, 8), :], la_s.at[k - 1], la_r.at[k - 1], peers_y[k - 1])
        for k in range(1, NY)
    ]
    for copy in copies:
        copy.wait_recv()
    pending += copies

    hops[2].wait_recv()
    hops[3].wait_recv()
    on_chip += [passed(2, left, last), passed(3, right, first)]

    leaf = own[...].reshape(N, N)
    (root,), (image,) = inverse_roots([leaf])
    leaves[0] = root
    leaves[1] = image
    rt[c, z, x] = leaves[:, rows_of(z, 16), :]
    copies = [
        send(rt.at[c, z, x], rt.at[c, z, x], b1_s.at[k], b1_r.at[k], peers_x[k]) for k in range(NX - 1)
    ]
    for copy in copies:
        copy.wait_recv()
    pending += copies
    copies_b = [send(rt.at[c, z], rt.at[c, z], b2_s.at[k], b2_r.at[k], peers_z[k]) for k in range(NZ - 1)]
    pending += copies_b

    hops[4].wait_recv()
    hops[5].wait_recv()
    on_chip += [passed(4, across, first), passed(5, across, last)]
    pending += hops[4:]
    pending += on_chip
    whole.wait_recv()
    for copy in on_chip:
        copy.wait_recv()

    @pl.loop(1, 5)
    def _(d):
        other = (2 * x + c - d + 8) % 8
        high, low = split(xall[other // NC, other % NC])
        part[d - 1] = gram_with(high, low).reshape(2, 64, N)

    copies = [
        send(part.at[:, :, rows_of((y + k) % NY, 8), :], rsy.at[k - 1], y_s.at[k - 1], y_r.at[k - 1], peers_y[k - 1])
        for k in range(1, NY)
    ]
    total = part[:, :, rows_of(y, 8), :]
    for k, copy in enumerate(copies):
        copy.wait_recv()
        total += rsy[k]
    pending += copies
    zsrc[...] = total.reshape(NZ, 8, N)
    copies = [
        send(zsrc.at[(z + k) % NZ], rsz.at[k - 1], z_s.at[k - 1], z_r.at[k - 1], peers_z[k - 1]) for k in range(1, NZ)
    ]
    total = zsrc[z]
    for k, copy in enumerate(copies):
        copy.wait_recv()
        total += rsz[k]
    pending += copies
    spot = rows_of(y, 8)
    kall[c, z, x, spot, :] = total
    copies = [
        send(kall.at[c, z, x, spot, :], kall.at[c, z, x, spot, :], p1_s.at[k], p1_r.at[k], peers_x[k])
        for k in range(NX - 1)
    ]
    for copy in copies:
        copy.wait_recv()
    pending += copies
    copies = [
        send(kall.at[c, z, :, spot, :], kall.at[c, z, :, spot, :], p2_s.at[k], p2_r.at[k], peers_z[k])
        for k in range(NZ - 1)
    ]
    for copy in copies:
        copy.wait_recv()
    pending += copies
    by_d = []
    for d in range(4):
        pair = pl.ds(2 * d, 2)
        by_d.append(
            [
                send(kall.at[c, pair, :, spot, :], kall.at[c, pair, :, spot, :], p3_s.at[d, k], p3_r.at[d, k], peers_y[k])
                for k in range(NY - 1)
            ]
        )
    for copy in copies_b:
        copy.wait_recv()
    swap = [send(rt.at[c], rt.at[c], b4_s, b4_r, partner)]
    for d in range(4):
        pair = pl.ds(2 * d, 2)
        for copy in by_d[d]:
            copy.wait_recv()
        pending += by_d[d]
        swap.append(send(kall.at[c, pair], kall.at[c, pair], p4_s.at[d], p4_r.at[d], partner))
    for copy in swap:
        copy.wait_recv()
    pending += swap
    for copy in pending:
        copy.wait_send()


def finish(tm_ref, xall, kall, rt, own, sk_ref, coef_ref, def_ref):
    tm = tm_ref[0]

    def at(o):
        g = (tm - o + 8) % 8
        return g // NC, g % NC

    def leaf(which, o):
        x, c = at(o)
        return rt[c, :, x, which].reshape(N, N)

    def stored(o, d):
        x, c = at(o)
        return jnp.concatenate([kall[c, 2 * d - 2, x], kall[c, 2 * d - 1, x]], 0)

    def block(a, b):
        return stored(a, b - a) if b - a <= 4 else stored(b, 8 - b + a).T

    def x_of(o):
        x, c = at(o)
        return xall[x, c]

    coef_ref[...], def_ref[...] = tree(
        functools.partial(leaf, 0),
        functools.partial(leaf, 1),
        block,
        own[...].reshape(N, N),
        lambda level: sk_ref[level],
        x_of,
    )


def body(snapshots, sketches):
    dma = pltpu.SemaphoreType.DMA
    vmem = pl.BlockSpec(memory_space=pltpu.VMEM)
    shapes = [(NX, NC, ROWS, N), (NC, NZ, NX, 64, N), (NC, NZ, NX, 2, 16, N), (2, 64, N)]
    counts = [6, 6, 7, 7, 7, 7, 7, 7, 3, 3, 7, 7, (4, 7), (4, 7), 4, 4, 7, 7, 7, 7, 7, 7, 3, 3, 7, 7]
    xall, kall, rt, own = pl.pallas_call(
        exchange,
        out_shape=[jax.ShapeDtypeStruct(s, F32) for s in shapes],
        in_specs=[vmem],
        out_specs=[vmem] * 4,
        scratch_shapes=[
            pltpu.VMEM((4, 2, 64, N), F32),
            pltpu.VMEM((NY - 1, 4, 2, 8, N), F32),
            pltpu.VMEM((NZ - 1, 8, N), F32),
            pltpu.VMEM((NZ, 8, N), F32),
            pltpu.VMEM((2, 64, N), F32),
            pltpu.VMEM((NY - 1, 2, 8, N), F32),
            pltpu.VMEM((NZ, 2, 8, N), F32),
            pltpu.VMEM((2, N, N), F32),
            *[dma(n if isinstance(n, tuple) else (n,)) for n in counts],
            dma,
            dma,
        ],
        compiler_params=pltpu.CompilerParams(collective_id=0, has_side_effects=True, vmem_limit_bytes=48 << 20),
        name="exchange",
    )(snapshots)
    tm = lax.axis_index("tm").astype(jnp.int32).reshape(1)
    return pl.pallas_call(
        finish,
        out_shape=[jax.ShapeDtypeStruct((N, N), F32), jax.ShapeDtypeStruct((ROWS, N), F32)],
        in_specs=[pl.BlockSpec(memory_space=pltpu.SMEM)] + [vmem] * 5,
        out_specs=[vmem] * 2,
        compiler_params=pltpu.CompilerParams(vmem_limit_bytes=60 << 20),
        name="finish",
    )(tm, xall, kall, rt, own, sketches)


def solution(mesh):
    placed = (P("row", "tm"), P())
    return jax.shard_map(
        body, mesh=mesh, in_specs=placed, out_specs=(P(None, "tm"), P("row", "tm")), check_vma=False
    )
```

```python
import functools

import jax
import jax.numpy as jnp
from jax import lax
from jax.experimental import pallas as pl
from jax.experimental.pallas import tpu as pltpu
from jax.sharding import PartitionSpec as P

BF, F32 = jnp.bfloat16, jnp.float32
MESH = pl.DeviceIdType.MESH
NX, NC, NY, NZ = 4, 2, 8, 8
N = 128
ROWS = 1024
HALF = ROWS // 2


def split(a):
    high = a.astype(BF)
    return high, (a - high.astype(F32)).astype(BF)


def mm(a, b):
    ah, al = split(a)
    bh, bl = split(b)
    left = jnp.concatenate([ah, ah, al], 1)
    right = jnp.concatenate([bh, bl, bh], 0)
    return jnp.dot(left, right, preferred_element_type=F32)


def identity():
    down = lax.broadcasted_iota(jnp.int32, (N, N), 0)
    across = lax.broadcasted_iota(jnp.int32, (N, N), 1)
    return jnp.where(down == across, 1.0, 0.0).astype(F32)


def inverse_roots(grams, want_image=True):
    one = identity()
    scales = [jnp.sqrt(jnp.sum(a * a, keepdims=True) + 1e-06) for a in grams]
    ts = [a / s for a, s in zip(grams, scales)]
    zs = ms = [1.5 * one - 0.5 * t for t in ts]
    ts = [mm(mm(t, m), m) for t, m in zip(ts, ms)]
    for step in range(1, 5):
        ms = [1.5 * one - 0.5 * t for t in ts]
        if step == 4 and not want_image:
            zs = [mm(z, m) for z, m in zip(zs, ms)]
        else:
            both = [mm(jnp.concatenate([t, z], 0), m) for t, z, m in zip(ts, zs, ms)]
            zs = [b[N:] for b in both]
            ts = [mm(b[:N], m) for b, m in zip(both, ms)]
    return [z / jnp.sqrt(s) for z, s in zip(zs, scales)], ts


def sketched(t_p, t_g, cross, sketch):
    top = jnp.concatenate([t_p, cross.T], 1)
    bottom = jnp.concatenate([cross, t_g], 1)
    gram = jnp.concatenate([top, bottom], 0)
    s = mm(gram, sketch)
    return s, mm(s.T, mm(gram, s))


def tree(root, image, block, own, sketch, x_of, gate):
    gate(0)
    r = [root(o) for o in range(8)]
    s0, a0, e0 = [], [], []
    for j in range(4):
        cross = mm(mm(r[2 * j], block(2 * j, 2 * j + 1)), r[2 * j + 1])
        s, a = sketched(image(2 * j + 1), image(2 * j), cross, sketch(0))
        s0.append(s)
        a0.append(a)
    for j in range(4):
        e0.append(jnp.concatenate([mm(r[2 * j + 1], s0[j][:N]), mm(r[2 * j], s0[j][N:])], 0))
    gate(1)
    gate(2)
    cross1 = []
    for j in range(0, 4, 2):
        upper = jnp.concatenate([block(2 * j + 1, 2 * j + 3), block(2 * j + 1, 2 * j + 2)], 1)
        lower = jnp.concatenate([block(2 * j, 2 * j + 3), block(2 * j, 2 * j + 2)], 1)
        cross1.append(mm(e0[j].T, mm(jnp.concatenate([upper, lower], 0), e0[j + 1])))
    r1, t1 = inverse_roots(a0)
    gate(3)
    s1, a1, e1 = [], [], []
    for j in range(2):
        cross = mm(mm(r1[2 * j], cross1[j]), r1[2 * j + 1])
        s, a = sketched(t1[2 * j + 1], t1[2 * j], cross, sketch(1))
        s1.append(s)
        a1.append(a)
    for j in range(2):
        upper = mm(e0[2 * j + 1], mm(r1[2 * j + 1], s1[j][:N]))
        lower = mm(e0[2 * j], mm(r1[2 * j], s1[j][N:]))
        e1.append(jnp.concatenate([upper, lower], 0))
    wide = [jnp.concatenate([block(a, b) for b in (7, 6, 5, 4)], 1) for a in (3, 2, 1, 0)]
    cross2 = mm(e1[0].T, mm(jnp.concatenate(wide, 0), e1[1]))
    near = jnp.concatenate([block(0, 3), block(0, 2), block(0, 1), own], 1)
    far = jnp.concatenate([block(0, 7), block(0, 6), block(0, 5), block(0, 4)], 1)
    w_far, w_near = mm(far, e1[1]), mm(near, e1[0])
    r2, t2 = inverse_roots(a1)
    s2, a2 = sketched(t2[1], t2[0], mm(mm(r2[0], cross2), r2[1]), sketch(2))
    h = mm(jnp.concatenate([mm(w_far, r2[1]), mm(w_near, r2[0])], 1), s2)
    upper = mm(e1[1], mm(r2[1], s2[:N]))
    lower = mm(e1[0], mm(r2[0], s2[N:]))
    x_all = jnp.concatenate([x_of(o) for o in range(7, -1, -1)], 1)
    base = mm(x_all, jnp.concatenate([upper, lower], 0))
    r3 = inverse_roots([a2], False)[0][0]
    coefficients = mm(h, r3).T
    return coefficients, x_of(0) - mm(base, mm(r3, coefficients))


def place():
    tm, row = lax.axis_index("tm"), lax.axis_index("row")
    c = tm % NC
    y, z = row % NY, row // NY
    return tm // NC, c, y + c * (z - y), z + c * (y - z)


def device(x, c, core, u, v):
    y, z = u + core * (v - u), v + core * (u - v)
    return (x * NC + c, z * NY + y)


def rows_of(index, count):
    return pl.ds(pl.multiple_of(index * count, count), count)


def step(x_hbm, sk_ref, coef_ref, def_ref, x_ref, xall, kall, rt, own, part, rsy, rsz, zsrc, lrow, lsy, lsz, leaves,
             g_s, g_r, c_s, c_r, y_s, y_r, z_s, z_r, p1_s, p1_r, p2_s, p2_r, p3_s, p3_r, p4_s, p4_r,
             ly_s, ly_r, lz_s, lz_r, la_s, la_r, b1_s, b1_r, b2_s, b2_r, b4_s, b4_r, load_s):
    x, c, u, v = place()
    tm = x * NC + c
    left, right, across = (x + 3) % NX, (x + 1) % NX, (x + 2) % NX
    peers_x = [device((x + k) % NX, c, c, u, v) for k in range(1, NX)]
    peers_y = [device(x, c, c, (u + k) % NY, v) for k in range(1, NY)]
    peers_z = [device(x, c, c, u, (v + k) % NZ) for k in range(1, NZ)]
    partner = device(x, 1 - c, c, u, v)

    barrier = pltpu.get_barrier_semaphore()
    everyone = peers_x + peers_y + peers_z + [partner]
    for peer in everyone:
        pl.semaphore_signal(barrier, inc=1, device_id=peer, device_id_type=MESH)
    load = pltpu.make_async_copy(x_hbm, x_ref, load_s)
    load.start()
    load.wait()

    mine = x_ref[...]
    xall[x, c] = mine
    mine_h, mine_l = split(mine)
    turned_h, turned_l = split(mine.T)
    turned = jnp.concatenate([turned_h, turned_h, turned_l], 1)

    def gram_with(high, low):
        return jnp.dot(turned, jnp.concatenate([high, low, high], 0), preferred_element_type=F32)

    lrow[...] = gram_with(mine_h, mine_l).reshape(2, 64, N)
    pl.semaphore_wait(barrier, len(everyone))

    def send(src, dst, s, r, peer):
        copy = pltpu.make_async_remote_copy(
            src_ref=src, dst_ref=dst, send_sem=s, recv_sem=r, device_id=peer, device_id_type=MESH
        )
        copy.start()
        return copy

    pending = []
    first, last = pl.ds(0, HALF), pl.ds(HALF, HALF)
    to_right, to_left = device(right, c, c, u, v), device(left, c, c, u, v)
    hops = []
    for k, (half, peer) in enumerate([(first, to_right), (last, to_left), (last, to_right), (first, to_left)]):
        hops.append(send(x_ref.at[half], xall.at[x, c, half], g_s.at[k], g_r.at[k], peer))
    pending += hops
    whole = send(x_ref, xall.at[x, c], c_s.at[6], c_r.at[6], partner)
    pending.append(whole)
    copies = [
        send(lrow.at[:, rows_of((u + k) % NY, 8), :], lsy.at[k - 1], ly_s.at[k - 1], ly_r.at[k - 1], peers_y[k - 1])
        for k in range(1, NY)
    ]
    total = lrow[:, rows_of(u, 8), :]
    for k, copy in enumerate(copies):
        copy.wait_recv()
        total += lsy[k]
    pending += copies
    lsz[NZ - 1] = total
    copies = [
        send(lsz.at[NZ - 1], lsz.at[k - 1], lz_s.at[k - 1], lz_r.at[k - 1], peers_z[k - 1])
        for k in range(1, NZ)
    ]

    def passed(k, source, half):
        return send(xall.at[source, c, half], xall.at[source, c, half], c_s.at[k], c_r.at[k], partner)

    hops[0].wait_recv()
    hops.append(send(xall.at[left, c, first], xall.at[left, c, first], g_s.at[4], g_r.at[4], to_right))
    hops[1].wait_recv()
    hops.append(send(xall.at[right, c, last], xall.at[right, c, last], g_s.at[5], g_r.at[5], to_left))
    on_chip = [passed(0, left, first), passed(1, right, last)]

    for copy in copies:
        copy.wait_recv()
    pending += copies
    total = jnp.zeros((2, 8, N), F32)
    for source in range(NZ):
        total += lsz[(v - source + NZ - 1) % NZ]
    own[:, rows_of(u, 8), :] = total
    copies = [
        send(own.at[:, rows_of(u, 8), :], own.at[:, rows_of(u, 8), :], la_s.at[k - 1], la_r.at[k - 1], peers_y[k - 1])
        for k in range(1, NY)
    ]
    for copy in copies:
        copy.wait_recv()
    pending += copies

    hops[2].wait_recv()
    hops[3].wait_recv()
    on_chip += [passed(2, left, last), passed(3, right, first)]

    leaf = own[...].reshape(N, N)
    (root,), (image,) = inverse_roots([leaf])
    leaves[0] = root
    leaves[1] = image
    rt[c, v, x] = leaves[:, rows_of(v, 16), :]
    copies = [
        send(rt.at[c, v, x], rt.at[c, v, x], b1_s.at[k], b1_r.at[k], peers_x[k]) for k in range(NX - 1)
    ]
    for copy in copies:
        copy.wait_recv()
    pending += copies
    copies_b = [send(rt.at[c, v], rt.at[c, v], b2_s.at[k], b2_r.at[k], peers_z[k]) for k in range(NZ - 1)]
    pending += copies_b

    hops[4].wait_recv()
    hops[5].wait_recv()
    on_chip += [passed(4, across, first), passed(5, across, last)]
    pending += hops[4:]
    pending += on_chip
    whole.wait_recv()
    for copy in on_chip:
        copy.wait_recv()

    @pl.loop(1, 5)
    def _(d):
        other = (2 * x + c - d + 8) % 8
        high, low = split(xall[other // NC, other % NC])
        part[d - 1] = gram_with(high, low).reshape(2, 64, N)

    copies = [
        send(part.at[:, :, rows_of((u + k) % NY, 8), :], rsy.at[k - 1], y_s.at[k - 1], y_r.at[k - 1], peers_y[k - 1])
        for k in range(1, NY)
    ]
    total = part[:, :, rows_of(u, 8), :]
    for k, copy in enumerate(copies):
        copy.wait_recv()
        total += rsy[k]
    pending += copies
    zsrc[...] = total.reshape(NZ, 8, N)
    copies = [
        send(zsrc.at[(v + k) % NZ], rsz.at[k - 1], z_s.at[k - 1], z_r.at[k - 1], peers_z[k - 1]) for k in range(1, NZ)
    ]
    total = zsrc[v]
    for k, copy in enumerate(copies):
        copy.wait_recv()
        total += rsz[k]
    pending += copies
    spot = rows_of(u, 8)
    kall[c, v, x, spot, :] = total
    copies = [
        send(kall.at[c, v, x, spot, :], kall.at[c, v, x, spot, :], p1_s.at[k], p1_r.at[k], peers_x[k])
        for k in range(NX - 1)
    ]
    for copy in copies:
        copy.wait_recv()
    pending += copies
    copies = [
        send(kall.at[c, v, :, spot, :], kall.at[c, v, :, spot, :], p2_s.at[k], p2_r.at[k], peers_z[k])
        for k in range(NZ - 1)
    ]
    for copy in copies:
        copy.wait_recv()
    pending += copies
    by_d = []
    for d in range(4):
        pair = pl.ds(2 * d, 2)
        by_d.append(
            [
                send(kall.at[c, pair, :, spot, :], kall.at[c, pair, :, spot, :], p3_s.at[d, k], p3_r.at[d, k], peers_y[k])
                for k in range(NY - 1)
            ]
        )
    for copy in copies_b:
        copy.wait_recv()
    swap = send(rt.at[c], rt.at[c], b4_s, b4_r, partner)
    pending.append(swap)

    def gate(d):
        pair = pl.ds(2 * d, 2)
        for copy in by_d[d]:
            copy.wait_recv()
        over = send(kall.at[c, pair], kall.at[c, pair], p4_s.at[d], p4_r.at[d], partner)
        if d == 0:
            swap.wait_recv()
        over.wait_recv()
        pending.append(over)
        pending.extend(by_d[d])

    def at(o):
        g = (tm - o + 8) % 8
        return g // NC, g % NC

    def leaf(which, o):
        gx, gc = at(o)
        return rt[gc, :, gx, which].reshape(N, N)

    def stored(o, d):
        gx, gc = at(o)
        return jnp.concatenate([kall[gc, 2 * d - 2, gx], kall[gc, 2 * d - 1, gx]], 0)

    def block(a, b):
        return stored(a, b - a) if b - a <= 4 else stored(b, 8 - b + a).T

    def x_of(o):
        gx, gc = at(o)
        return xall[gx, gc]

    coef_ref[...], def_ref[...] = tree(
        functools.partial(leaf, 0),
        functools.partial(leaf, 1),
        block,
        own[...].reshape(N, N),
        lambda level: sk_ref[level],
        x_of,
        gate,
    )
    for copy in pending:
        copy.wait_send()


def body(snapshots, sketches):
    dma = pltpu.SemaphoreType.DMA
    vmem = pl.BlockSpec(memory_space=pltpu.VMEM)
    counts = [6, 6, 7, 7, 7, 7, 7, 7, 3, 3, 7, 7, (4, 7), (4, 7), 4, 4, 7, 7, 7, 7, 7, 7, 3, 3, 7, 7]
    shapes = [
        (ROWS, N),
        (NX, NC, ROWS, N),
        (NC, NZ, NX, 64, N),
        (NC, NZ, NX, 2, 16, N),
        (2, 64, N),
        (4, 2, 64, N),
        (NY - 1, 4, 2, 8, N),
        (NZ - 1, 8, N),
        (NZ, 8, N),
        (2, 64, N),
        (NY - 1, 2, 8, N),
        (NZ, 2, 8, N),
        (2, N, N),
    ]
    return pl.pallas_call(
        step,
        out_shape=[jax.ShapeDtypeStruct((N, N), F32), jax.ShapeDtypeStruct((ROWS, N), F32)],
        in_specs=[pl.BlockSpec(memory_space=pl.ANY), vmem],
        out_specs=[vmem] * 2,
        scratch_shapes=[
            *[pltpu.VMEM(s, F32) for s in shapes],
            *[dma(n if isinstance(n, tuple) else (n,)) for n in counts],
            dma,
            dma,
            dma,
        ],
        compiler_params=pltpu.CompilerParams(collective_id=0, has_side_effects=True, vmem_limit_bytes=60 << 20),
        name="step",
    )(snapshots, sketches)


def solution(mesh):
    placed = (P("row", "tm"), P())
    return jax.shard_map(
        body, mesh=mesh, in_specs=placed, out_specs=(P(None, "tm"), P("row", "tm")), check_vma=False
    )
```

```python
import functools

import jax
import jax.numpy as jnp
from jax import lax
from jax.experimental import pallas as pl
from jax.experimental.pallas import tpu as pltpu
from jax.sharding import PartitionSpec as P

BF, F32 = jnp.bfloat16, jnp.float32
MESH = pl.DeviceIdType.MESH
NX, NC, NY, NZ = 4, 2, 8, 8
N = 128
ROWS = 1024
SPLIT = 384


def split(a):
    high = a.astype(BF)
    return high, (a - high.astype(F32)).astype(BF)


def mm(a, b):
    ah, al = split(a)
    bh, bl = split(b)
    left = jnp.concatenate([ah, ah, al], 1)
    right = jnp.concatenate([bh, bl, bh], 0)
    return jnp.dot(left, right, preferred_element_type=F32)


def identity():
    down = lax.broadcasted_iota(jnp.int32, (N, N), 0)
    across = lax.broadcasted_iota(jnp.int32, (N, N), 1)
    return jnp.where(down == across, 1.0, 0.0).astype(F32)


def inverse_roots(grams, want_image=True):
    one = identity()
    scales = [jnp.sqrt(jnp.sum(a * a, keepdims=True) + 1e-06) for a in grams]
    ts = [a / s for a, s in zip(grams, scales)]
    zs = ms = [1.5 * one - 0.5 * t for t in ts]
    ts = [mm(mm(t, m), m) for t, m in zip(ts, ms)]
    for step in range(1, 5):
        ms = [1.5 * one - 0.5 * t for t in ts]
        if step == 4 and not want_image:
            zs = [mm(z, m) for z, m in zip(zs, ms)]
        else:
            both = [mm(jnp.concatenate([t, z], 0), m) for t, z, m in zip(ts, zs, ms)]
            zs = [b[N:] for b in both]
            ts = [mm(b[:N], m) for b, m in zip(both, ms)]
    return [z / jnp.sqrt(s) for z, s in zip(zs, scales)], ts


def sketched(t_p, t_g, cross, sketch):
    top = jnp.concatenate([t_p, cross.T], 1)
    bottom = jnp.concatenate([cross, t_g], 1)
    gram = jnp.concatenate([top, bottom], 0)
    s = mm(gram, sketch)
    return s, mm(s.T, mm(gram, s))


def tree(root, image, block, own, sketch, x_of, gate):
    gate(0)
    r = [root(o) for o in range(8)]
    s0, a0, e0 = [], [], []
    for j in range(4):
        cross = mm(mm(r[2 * j], block(2 * j, 2 * j + 1)), r[2 * j + 1])
        s, a = sketched(image(2 * j + 1), image(2 * j), cross, sketch(0))
        s0.append(s)
        a0.append(a)
    for j in range(4):
        e0.append(jnp.concatenate([mm(r[2 * j + 1], s0[j][:N]), mm(r[2 * j], s0[j][N:])], 0))
    gate(1)
    gate(2)
    cross1 = []
    for j in range(0, 4, 2):
        upper = jnp.concatenate([block(2 * j + 1, 2 * j + 3), block(2 * j + 1, 2 * j + 2)], 1)
        lower = jnp.concatenate([block(2 * j, 2 * j + 3), block(2 * j, 2 * j + 2)], 1)
        cross1.append(mm(e0[j].T, mm(jnp.concatenate([upper, lower], 0), e0[j + 1])))
    r1, t1 = inverse_roots(a0)
    gate(3)
    s1, a1, e1 = [], [], []
    for j in range(2):
        cross = mm(mm(r1[2 * j], cross1[j]), r1[2 * j + 1])
        s, a = sketched(t1[2 * j + 1], t1[2 * j], cross, sketch(1))
        s1.append(s)
        a1.append(a)
    for j in range(2):
        upper = mm(e0[2 * j + 1], mm(r1[2 * j + 1], s1[j][:N]))
        lower = mm(e0[2 * j], mm(r1[2 * j], s1[j][N:]))
        e1.append(jnp.concatenate([upper, lower], 0))
    wide = [jnp.concatenate([block(a, b) for b in (7, 6, 5, 4)], 1) for a in (3, 2, 1, 0)]
    cross2 = mm(e1[0].T, mm(jnp.concatenate(wide, 0), e1[1]))
    near = jnp.concatenate([block(0, 3), block(0, 2), block(0, 1), own], 1)
    far = jnp.concatenate([block(0, 7), block(0, 6), block(0, 5), block(0, 4)], 1)
    w_far, w_near = mm(far, e1[1]), mm(near, e1[0])
    r2, t2 = inverse_roots(a1)
    s2, a2 = sketched(t2[1], t2[0], mm(mm(r2[0], cross2), r2[1]), sketch(2))
    h = mm(jnp.concatenate([mm(w_far, r2[1]), mm(w_near, r2[0])], 1), s2)
    upper = mm(e1[1], mm(r2[1], s2[:N]))
    lower = mm(e1[0], mm(r2[0], s2[N:]))
    x_all = jnp.concatenate([x_of(o) for o in range(7, -1, -1)], 1)
    base = mm(x_all, jnp.concatenate([upper, lower], 0))
    r3 = inverse_roots([a2], False)[0][0]
    turned = mm(h, r3)
    return turned, mm(base, mm(r3, turned.T))


def place():
    tm, row = lax.axis_index("tm"), lax.axis_index("row")
    c = tm % NC
    y, z = row % NY, row // NY
    return tm // NC, c, y + c * (z - y), z + c * (y - z)


def device(x, c, core, u, v):
    y, z = u + core * (v - u), v + core * (u - v)
    return (x * NC + c, z * NY + y)


def rows_of(index, count):
    return pl.ds(pl.multiple_of(index * count, count), count)


def step(x_hbm, sk_ref, coef_ref, def_ref, x_ref, xall, kall, rt, own, part, rsy, rsz, zsrc, lrow, lsy, lsz, leaves,
             g_s, g_r, c_s, c_r, y_s, y_r, z_s, z_r, p1_s, p1_r, p2_s, p2_r, p3_s, p3_r, p4_s, p4_r,
             ly_s, ly_r, lz_s, lz_r, la_s, la_r, b1_s, b1_r, b2_s, b2_r, b4_s, b4_r, load_s):
    x, c, u, v = place()
    tm = x * NC + c
    left, right, across = (x + 3) % NX, (x + 1) % NX, (x + 2) % NX
    peers_x = [device((x + k) % NX, c, c, u, v) for k in range(1, NX)]
    peers_y = [device(x, c, c, (u + k) % NY, v) for k in range(1, NY)]
    peers_z = [device(x, c, c, u, (v + k) % NZ) for k in range(1, NZ)]
    partner = device(x, 1 - c, c, u, v)

    barrier = pltpu.get_barrier_semaphore()
    everyone = peers_x + peers_y + peers_z + [partner]
    for peer in everyone:
        pl.semaphore_signal(barrier, inc=1, device_id=peer, device_id_type=MESH)
    load = pltpu.make_async_copy(x_hbm, x_ref, load_s)
    load.start()
    load.wait()

    mine = x_ref[...]
    xall[x, c] = mine
    mine_h, mine_l = split(mine)
    turned_h, turned_l = split(mine.T)
    turned = jnp.concatenate([turned_h, turned_h, turned_l], 1)

    def gram_with(high, low):
        return jnp.dot(turned, jnp.concatenate([high, low, high], 0), preferred_element_type=F32)

    lrow[...] = gram_with(mine_h, mine_l).reshape(2, 64, N)
    pl.semaphore_wait(barrier, len(everyone))

    def send(src, dst, s, r, peer):
        copy = pltpu.make_async_remote_copy(
            src_ref=src, dst_ref=dst, send_sem=s, recv_sem=r, device_id=peer, device_id_type=MESH
        )
        copy.start()
        return copy

    pending = []
    first, last = pl.ds(0, SPLIT), pl.ds(SPLIT, ROWS - SPLIT)
    to_right, to_left = device(right, c, c, u, v), device(left, c, c, u, v)

    def hop(k, source, part_of, peer, src=None):
        src = xall.at[source, c, part_of] if src is None else src
        copy = send(src, xall.at[source, c, part_of], g_s.at[k], g_r.at[k], peer)
        pending.append(copy)
        return copy

    def passed(k, source, part_of):
        here = xall.at[source, c, part_of]
        copy = send(here, here, c_s.at[k], c_r.at[k], partner)
        pending.append(copy)
        return copy

    hop0 = hop(0, x, first, to_right, x_ref.at[first])
    hop1 = hop(1, x, last, to_left, x_ref.at[last])
    hop2 = hop(2, x, last, to_right, x_ref.at[last])
    whole = send(x_ref, xall.at[x, c], c_s.at[6], c_r.at[6], partner)
    pending.append(whole)
    copies = [
        send(lrow.at[:, rows_of((u + k) % NY, 8), :], lsy.at[k - 1], ly_s.at[k - 1], ly_r.at[k - 1], peers_y[k - 1])
        for k in range(1, NY)
    ]
    total = lrow[:, rows_of(u, 8), :]
    for k, copy in enumerate(copies):
        copy.wait_recv()
        total += lsy[k]
    pending += copies
    lsz[NZ - 1] = total
    copies = [
        send(lsz.at[NZ - 1], lsz.at[k - 1], lz_s.at[k - 1], lz_r.at[k - 1], peers_z[k - 1])
        for k in range(1, NZ)
    ]

    hop0.wait_recv()
    hop4 = hop(4, left, first, to_right)
    chip0 = passed(0, left, first)

    for copy in copies:
        copy.wait_recv()
    pending += copies
    total = jnp.zeros((2, 8, N), F32)
    for source in range(NZ):
        total += lsz[(v - source + NZ - 1) % NZ]
    own[:, rows_of(u, 8), :] = total
    copies = [
        send(own.at[:, rows_of(u, 8), :], own.at[:, rows_of(u, 8), :], la_s.at[k - 1], la_r.at[k - 1], peers_y[k - 1])
        for k in range(1, NY)
    ]
    hop1.wait_recv()
    hop5 = hop(5, right, last, to_left)
    hop3 = hop(3, x, first, to_left, x_ref.at[first])
    chip1 = passed(1, right, last)
    for copy in copies:
        copy.wait_recv()
    pending += copies

    leaf = own[...].reshape(N, N)
    (root,), (image,) = inverse_roots([leaf])
    leaves[0] = root
    leaves[1] = image
    rt[c, v, x] = leaves[:, rows_of(v, 16), :]
    copies_x = [
        send(rt.at[c, v, x], rt.at[c, v, x], b1_s.at[k], b1_r.at[k], peers_x[k]) for k in range(NX - 1)
    ]
    pending += copies_x
    hop2.wait_recv()
    chip2 = passed(2, left, last)

    def cross_gram(d):
        other = (2 * x + c - d + 8) % 8
        high, low = split(xall[other // NC, other % NC])
        part[d - 1] = gram_with(high, low).reshape(2, 64, N)

    def first_sum(half):
        pair = pl.ds(2 * half, 2)
        return [
            send(
                part.at[pair, :, rows_of((u + k) % NY, 8), :],
                rsy.at[k - 1, pair],
                y_s.at[half, k - 1],
                y_r.at[half, k - 1],
                peers_y[k - 1],
            )
            for k in range(1, NY)
        ]

    whole.wait_recv()
    chip0.wait_recv()
    chip2.wait_recv()
    cross_gram(1)
    cross_gram(2)
    sums = [first_sum(0)]
    hop4.wait_recv()
    chip4 = passed(4, across, first)
    hop5.wait_recv()
    chip5 = passed(5, across, last)
    for copy in copies_x:
        copy.wait_recv()
    copies_b = [send(rt.at[c, v], rt.at[c, v], b2_s.at[k], b2_r.at[k], peers_z[k]) for k in range(NZ - 1)]
    pending += copies_b
    chip4.wait_recv()
    chip5.wait_recv()
    cross_gram(3)
    cross_gram(4)
    sums.append(first_sum(1))
    hop3.wait_recv()
    chip3 = passed(3, right, first)
    pending += sums[0] + sums[1]
    total = part[:, :, rows_of(u, 8), :]
    for k in range(NY - 1):
        sums[0][k].wait_recv()
        sums[1][k].wait_recv()
        total += rsy[k]
    zsrc[...] = total.reshape(NZ, 8, N)
    copies = [
        send(zsrc.at[(v + k) % NZ], rsz.at[k - 1], z_s.at[k - 1], z_r.at[k - 1], peers_z[k - 1]) for k in range(1, NZ)
    ]
    total = zsrc[v]
    for k, copy in enumerate(copies):
        copy.wait_recv()
        total += rsz[k]
    pending += copies
    spot = rows_of(u, 8)
    kall[c, v, x, spot, :] = total
    copies = [
        send(kall.at[c, v, x, spot, :], kall.at[c, v, x, spot, :], p1_s.at[k], p1_r.at[k], peers_x[k])
        for k in range(NX - 1)
    ]
    for copy in copies:
        copy.wait_recv()
    pending += copies
    copies = [
        send(kall.at[c, v, :, spot, :], kall.at[c, v, :, spot, :], p2_s.at[k], p2_r.at[k], peers_z[k])
        for k in range(NZ - 1)
    ]
    for copy in copies:
        copy.wait_recv()
    pending += copies
    by_d = []
    for d in range(4):
        pair = pl.ds(2 * d, 2)
        by_d.append(
            [
                send(kall.at[c, pair, :, spot, :], kall.at[c, pair, :, spot, :], p3_s.at[d, k], p3_r.at[d, k], peers_y[k])
                for k in range(NY - 1)
            ]
        )
    for copy in copies_b:
        copy.wait_recv()
    swap = send(rt.at[c], rt.at[c], b4_s, b4_r, partner)
    pending.append(swap)

    def gate(d):
        pair = pl.ds(2 * d, 2)
        for copy in by_d[d]:
            copy.wait_recv()
        over = send(kall.at[c, pair], kall.at[c, pair], p4_s.at[d], p4_r.at[d], partner)
        if d == 0:
            swap.wait_recv()
        if d == 3:
            chip1.wait_recv()
            chip3.wait_recv()
        over.wait_recv()
        pending.append(over)
        pending.extend(by_d[d])

    def at(o):
        g = (tm - o + 8) % 8
        return g // NC, g % NC

    def leaf(which, o):
        gx, gc = at(o)
        return rt[gc, :, gx, which].reshape(N, N)

    def stored(o, d):
        gx, gc = at(o)
        return jnp.concatenate([kall[gc, 2 * d - 2, gx], kall[gc, 2 * d - 1, gx]], 0)

    def block(a, b):
        return stored(a, b - a) if b - a <= 4 else stored(b, 8 - b + a).T

    def x_of(o):
        gx, gc = at(o)
        return xall[gx, gc]

    coef_ref[...], def_ref[...] = tree(
        functools.partial(leaf, 0),
        functools.partial(leaf, 1),
        block,
        own[...].reshape(N, N),
        lambda level: sk_ref[level],
        x_of,
        gate,
    )
    for copy in pending:
        copy.wait_send()


def body(snapshots, sketches):
    dma = pltpu.SemaphoreType.DMA
    vmem = pl.BlockSpec(memory_space=pltpu.VMEM)
    counts = [6, 6, 7, 7, (2, 7), (2, 7), 7, 7, 3, 3, 7, 7, (4, 7), (4, 7), 4, 4, 7, 7, 7, 7, 7, 7, 3, 3, 7, 7]
    shapes = [
        (ROWS, N),
        (NX, NC, ROWS, N),
        (NC, NZ, NX, 64, N),
        (NC, NZ, NX, 2, 16, N),
        (2, 64, N),
        (4, 2, 64, N),
        (NY - 1, 4, 2, 8, N),
        (NZ - 1, 8, N),
        (NZ, 8, N),
        (2, 64, N),
        (NY - 1, 2, 8, N),
        (NZ, 2, 8, N),
        (2, N, N),
    ]
    turned, removed = pl.pallas_call(
        step,
        out_shape=[jax.ShapeDtypeStruct((N, N), F32), jax.ShapeDtypeStruct((ROWS, N), F32)],
        in_specs=[pl.BlockSpec(memory_space=pl.ANY), vmem],
        out_specs=[vmem] * 2,
        scratch_shapes=[
            *[pltpu.VMEM(s, F32) for s in shapes],
            *[dma(n if isinstance(n, tuple) else (n,)) for n in counts],
            dma,
            dma,
            dma,
        ],
        compiler_params=pltpu.CompilerParams(collective_id=0, has_side_effects=True, vmem_limit_bytes=60 << 20),
        name="step",
    )(snapshots, sketches)
    return turned.T, snapshots - removed


def solution(mesh):
    placed = (P("row", "tm"), P())
    return jax.shard_map(
        body, mesh=mesh, in_specs=placed, out_specs=(P(None, "tm"), P("row", "tm")), check_vma=False
    )
```

```python
import jax
import jax.numpy as jnp
from jax import lax
from jax.experimental import pallas as pl
from jax.experimental.pallas import tpu as pltpu
from jax.sharding import PartitionSpec as P

BF, F32 = jnp.bfloat16, jnp.float32
MESH = pl.DeviceIdType.MESH
NX, NC, NY, NZ = 4, 2, 8, 8
N = 128
ROWS = 1024
SPLIT = 384


def split(a):
    high = a.astype(BF)
    return high, (a - high.astype(F32)).astype(BF)


def mm(a, b):
    ah, al = split(a)
    bh, bl = split(b)
    left = jnp.concatenate([ah, ah, al], 1)
    right = jnp.concatenate([bh, bl, bh], 0)
    return jnp.dot(left, right, preferred_element_type=F32)


def identity():
    down = lax.broadcasted_iota(jnp.int32, (N, N), 0)
    across = lax.broadcasted_iota(jnp.int32, (N, N), 1)
    return jnp.where(down == across, 1.0, 0.0).astype(F32)


def inverse_roots(grams, want_image=True):
    one = identity()
    scales = [jnp.sqrt(jnp.sum(a * a, keepdims=True) + 1e-06) for a in grams]
    ts = [a / s for a, s in zip(grams, scales)]
    zs = ms = [1.5 * one - 0.5 * t for t in ts]
    ts = [mm(mm(t, m), m) for t, m in zip(ts, ms)]
    for step in range(1, 5):
        ms = [1.5 * one - 0.5 * t for t in ts]
        if step == 4 and not want_image:
            zs = [mm(z, m) for z, m in zip(zs, ms)]
        else:
            both = [mm(jnp.concatenate([t, z], 0), m) for t, z, m in zip(ts, zs, ms)]
            zs = [b[N:] for b in both]
            ts = [mm(b[:N], m) for b, m in zip(both, ms)]
    return [z / jnp.sqrt(s) for z, s in zip(zs, scales)], ts


def sketched(t_p, t_g, cross, sketch):
    top = jnp.concatenate([t_p, cross.T], 1)
    bottom = jnp.concatenate([cross, t_g], 1)
    gram = jnp.concatenate([top, bottom], 0)
    s = mm(gram, sketch)
    return s, mm(s.T, mm(gram, s))


def tree(root, image, block, own, sketch, x_of, gate):
    gate(0)
    r = [root(o) for o in range(8)]
    s0, a0, e0 = [], [], []
    for j in range(4):
        cross = mm(mm(r[2 * j], block(2 * j, 2 * j + 1)), r[2 * j + 1])
        s, a = sketched(image(2 * j + 1), image(2 * j), cross, sketch(0))
        s0.append(s)
        a0.append(a)
    for j in range(4):
        e0.append(jnp.concatenate([mm(r[2 * j + 1], s0[j][:N]), mm(r[2 * j], s0[j][N:])], 0))
    r1, t1 = inverse_roots(a0)
    gate(1)
    gate(2)
    cross1 = []
    for j in range(0, 4, 2):
        upper = jnp.concatenate([block(2 * j + 1, 2 * j + 3), block(2 * j + 1, 2 * j + 2)], 1)
        lower = jnp.concatenate([block(2 * j, 2 * j + 3), block(2 * j, 2 * j + 2)], 1)
        cross1.append(mm(e0[j].T, mm(jnp.concatenate([upper, lower], 0), e0[j + 1])))
    s1, a1, e1 = [], [], []
    for j in range(2):
        cross = mm(mm(r1[2 * j], cross1[j]), r1[2 * j + 1])
        s, a = sketched(t1[2 * j + 1], t1[2 * j], cross, sketch(1))
        s1.append(s)
        a1.append(a)
    for j in range(2):
        upper = mm(e0[2 * j + 1], mm(r1[2 * j + 1], s1[j][:N]))
        lower = mm(e0[2 * j], mm(r1[2 * j], s1[j][N:]))
        e1.append(jnp.concatenate([upper, lower], 0))
    r2, t2 = inverse_roots(a1)
    gate(3)
    wide = [jnp.concatenate([block(a, b) for b in (7, 6, 5, 4)], 1) for a in (3, 2, 1, 0)]
    cross2 = mm(e1[0].T, mm(jnp.concatenate(wide, 0), e1[1]))
    near = jnp.concatenate([block(0, 3), block(0, 2), block(0, 1), own], 1)
    far = jnp.concatenate([block(0, 7), block(0, 6), block(0, 5), block(0, 4)], 1)
    w_far, w_near = mm(far, e1[1]), mm(near, e1[0])
    s2, a2 = sketched(t2[1], t2[0], mm(mm(r2[0], cross2), r2[1]), sketch(2))
    h = mm(jnp.concatenate([mm(w_far, r2[1]), mm(w_near, r2[0])], 1), s2)
    upper = mm(e1[1], mm(r2[1], s2[:N]))
    lower = mm(e1[0], mm(r2[0], s2[N:]))
    x_all = jnp.concatenate([x_of(o) for o in range(7, -1, -1)], 1)
    base = mm(x_all, jnp.concatenate([upper, lower], 0))
    r3 = inverse_roots([a2], False)[0][0]
    turned = mm(h, r3)
    return turned, mm(base, mm(r3, turned.T))


def place():
    tm, row = lax.axis_index("tm"), lax.axis_index("row")
    c = tm % NC
    y, z = row % NY, row // NY
    return tm // NC, c, y + c * (z - y), z + c * (y - z)


def device(x, c, core, u, v):
    y, z = u + core * (v - u), v + core * (u - v)
    return (x * NC + c, z * NY + y)


def rows_of(index, count):
    return pl.ds(pl.multiple_of(index * count, count), count)


def step(x_hbm, sk_ref, coef_ref, def_ref, x_ref, xall, kall, leaves, roots, part, rsy, rsz, lrow, lsy, lsz,
         g_s, g_r, c_s, c_r, y_s, y_r, z_s, z_r, p1_s, p1_r, p3_s, p3_r, p4_s, p4_r,
         ly_s, ly_r, lz_s, lz_r, b1_s, b1_r, b2_s, b2_r, b4_s, b4_r, load_s):
    x, c, u, v = place()
    tm = x * NC + c
    left, right, across = (x + 3) % NX, (x + 1) % NX, (x + 2) % NX
    peers_x = [device((x + k) % NX, c, c, u, v) for k in range(1, NX)]
    peers_y = [device(x, c, c, (u + k) % NY, v) for k in range(1, NY)]
    peers_z = [device(x, c, c, u, (v + k) % NZ) for k in range(1, NZ)]
    partner = device(x, 1 - c, c, u, v)

    barrier = pltpu.get_barrier_semaphore()
    everyone = peers_x + peers_y + peers_z + [partner]
    for peer in everyone:
        pl.semaphore_signal(barrier, inc=1, device_id=peer, device_id_type=MESH)
    load = pltpu.make_async_copy(x_hbm, x_ref, load_s)
    load.start()
    load.wait()

    mine = x_ref[...]
    xall[x, c] = mine
    mine_h, mine_l = split(mine)
    turned_h, turned_l = split(mine.T)
    turned = jnp.concatenate([turned_h, turned_h, turned_l], 1)

    def gram_with(high, low):
        return jnp.dot(turned, jnp.concatenate([high, low, high], 0), preferred_element_type=F32)

    lrow[...] = gram_with(mine_h, mine_l).reshape(2, 64, N)
    pl.semaphore_wait(barrier, len(everyone))

    def send(src, dst, s, r, peer):
        copy = pltpu.make_async_remote_copy(
            src_ref=src, dst_ref=dst, send_sem=s, recv_sem=r, device_id=peer, device_id_type=MESH
        )
        copy.start()
        return copy

    pending = []
    first, last = pl.ds(0, SPLIT), pl.ds(SPLIT, ROWS - SPLIT)
    to_right, to_left = device(right, c, c, u, v), device(left, c, c, u, v)

    def hop(k, source, part_of, peer, src=None):
        src = xall.at[source, c, part_of] if src is None else src
        copy = send(src, xall.at[source, c, part_of], g_s.at[k], g_r.at[k], peer)
        pending.append(copy)
        return copy

    def passed(k, source, part_of):
        here = xall.at[source, c, part_of]
        copy = send(here, here, c_s.at[k], c_r.at[k], partner)
        pending.append(copy)
        return copy

    hop0 = hop(0, x, first, to_right, x_ref.at[first])
    hop1 = hop(1, x, last, to_left, x_ref.at[last])
    hop2 = hop(2, x, last, to_right, x_ref.at[last])
    whole = send(x_ref, xall.at[x, c], c_s.at[6], c_r.at[6], partner)
    pending.append(whole)
    copies = [
        send(lrow.at[:, rows_of((u + k) % NY, 8), :], lsy.at[k - 1], ly_s.at[k - 1], ly_r.at[k - 1], peers_y[k - 1])
        for k in range(1, NY)
    ]
    total = lrow[:, rows_of(u, 8), :]
    for k, copy in enumerate(copies):
        copy.wait_recv()
        total += lsy[k]
    pending += copies
    lsz[NZ - 1] = total
    copies = [
        send(lsz.at[NZ - 1], lsz.at[k - 1], lz_s.at[k - 1], lz_r.at[k - 1], peers_z[k - 1])
        for k in range(1, NZ)
    ]

    hop0.wait_recv()
    hop4 = hop(4, left, first, to_right)
    chip0 = passed(0, left, first)

    def in_order(slots):
        total = slots[(v + NZ - 1) % NZ]
        for source in range(1, NZ):
            total += slots[(v - source + NZ - 1) % NZ]
        return total

    def received(copies):
        for copy in copies:
            copy.wait_recv()
        pending.extend(copies)

    spot = rows_of(u, 8)

    def to_line(src, dst, s, r, peers):
        return [send(src, dst, s.at[k], r.at[k], peer) for k, peer in enumerate(peers)]

    def same(ref, s, r, peers):
        return to_line(ref, ref, s, r, peers)

    received(copies)
    leaves[c, :, x, spot, :] = in_order(lsz)
    leaf_x = same(leaves.at[c, :, x, spot, :], b1_s, b1_r, peers_x)
    hop1.wait_recv()
    hop5 = hop(5, right, last, to_left)
    hop3 = hop(3, x, first, to_left, x_ref.at[first])
    chip1 = passed(1, right, last)
    hop2.wait_recv()
    chip2 = passed(2, left, last)

    def cross_gram(d):
        other = (2 * x + c - d + 8) % 8
        high, low = split(xall[other // NC, other % NC])
        part[d - 1] = gram_with(high, low).reshape(2, 64, N)

    def scatter(half):
        pair = pl.ds(2 * half, 2)
        return [
            send(
                part.at[pair, :, rows_of((u + k) % NY, 8), :],
                rsy.at[half, k - 1],
                y_s.at[half, k - 1],
                y_r.at[half, k - 1],
                peers_y[k - 1],
            )
            for k in range(1, NY)
        ]

    def spread(half, copies):
        received(copies)
        total = part[2 * half : 2 * half + 2, :, spot, :]
        for k in range(NY - 1):
            total += rsy[half, k]
        rsz[half, NZ - 1] = total.reshape(4, 8, N)
        return [
            send(rsz.at[half, NZ - 1], rsz.at[half, k], z_s.at[half, k], z_r.at[half, k], peers_z[k])
            for k in range(NZ - 1)
        ]

    def along_x(half, copies):
        received(copies)
        quad = pl.ds(4 * half, 4)
        kall[c, quad, x, spot, :] = in_order(rsz.at[half])
        return same(kall.at[c, quad, x, spot, :], p1_s.at[half], p1_r.at[half], peers_x)

    def along_u(half, copies):
        received(copies)
        return [
            same(kall.at[c, pl.ds(2 * d, 2), :, spot, :], p3_s.at[d], p3_r.at[d], peers_y)
            for d in (2 * half, 2 * half + 1)
        ]

    def swap(d, copies):
        received(copies)
        pair = pl.ds(2 * d, 2)
        over = send(kall.at[c, pair], kall.at[c, pair], p4_s.at[d], p4_r.at[d], partner)
        pending.append(over)
        return over

    whole.wait_recv()
    chip0.wait_recv()
    chip2.wait_recv()
    cross_gram(1)
    cross_gram(2)
    near = scatter(0)
    hop4.wait_recv()
    chip4 = passed(4, across, first)
    hop5.wait_recv()
    chip5 = passed(5, across, last)
    received(leaf_x)
    leaf_u = same(leaves.at[c, :, :, spot, :], b2_s, b2_r, peers_y)
    chip4.wait_recv()
    chip5.wait_recv()
    cross_gram(3)
    cross_gram(4)
    far = scatter(1)
    near = spread(0, near)
    far = spread(1, far)
    near = along_x(0, near)
    received(leaf_u)
    over = send(leaves.at[c], leaves.at[c], b4_s, b4_r, partner)
    pending.append(over)
    near = along_u(0, near)
    far = along_x(1, far)
    over.wait_recv()

    def leaf(o):
        gx, gc = at(o)
        return jnp.concatenate([leaves[gc, 0, gx], leaves[gc, 1, gx]], 0)

    def at(o):
        g = (tm - o + 8) % 8
        return g // NC, g % NC

    for o in (0, 4):
        some, images = inverse_roots([leaf(o + i) for i in range(4)])
        for i in range(4):
            roots[o + i] = some[i]
            roots[8 + o + i] = images[i]
        if o == 0:
            far = along_u(1, far)
    hop3.wait_recv()
    chip3 = passed(3, right, first)
    overs = [swap(0, near[0]), swap(1, near[1])]

    def gate(d):
        if d == 2:
            overs.extend([swap(2, far[0]), swap(3, far[1])])
        if d == 3:
            chip1.wait_recv()
            chip3.wait_recv()
        overs[d].wait_recv()

    def stored(o, d):
        gx, gc = at(o)
        return jnp.concatenate([kall[gc, 2 * d - 2, gx], kall[gc, 2 * d - 1, gx]], 0)

    def block(a, b):
        return stored(a, b - a) if b - a <= 4 else stored(b, 8 - b + a).T

    def x_of(o):
        gx, gc = at(o)
        return xall[gx, gc]

    coef_ref[...], def_ref[...] = tree(
        lambda o: roots[o],
        lambda o: roots[8 + o],
        block,
        leaf(0),
        lambda level: sk_ref[level],
        x_of,
        gate,
    )
    for copy in pending:
        copy.wait_send()


def body(snapshots, sketches):
    dma = pltpu.SemaphoreType.DMA
    vmem = pl.BlockSpec(memory_space=pltpu.VMEM)
    counts = [6, 6, 7, 7, (2, 7), (2, 7), (2, 7), (2, 7), (2, 3), (2, 3), (4, 7), (4, 7), 4, 4, 7, 7, 7, 7, 3, 3, 7, 7]
    shapes = [
        (ROWS, N),
        (NX, NC, ROWS, N),
        (NC, NZ, NX, 64, N),
        (NC, 2, NX, 64, N),
        (16, N, N),
        (4, 2, 64, N),
        (2, NY - 1, 2, 2, 8, N),
        (2, NZ, 4, 8, N),
        (2, 64, N),
        (NY - 1, 2, 8, N),
        (NZ, 2, 8, N),
    ]
    turned, removed = pl.pallas_call(
        step,
        out_shape=[jax.ShapeDtypeStruct((N, N), F32), jax.ShapeDtypeStruct((ROWS, N), F32)],
        in_specs=[pl.BlockSpec(memory_space=pl.ANY), vmem],
        out_specs=[vmem] * 2,
        scratch_shapes=[
            *[pltpu.VMEM(s, F32) for s in shapes],
            *[dma(n if isinstance(n, tuple) else (n,)) for n in counts],
            dma,
            dma,
            dma,
        ],
        compiler_params=pltpu.CompilerParams(collective_id=0, has_side_effects=True, vmem_limit_bytes=60 << 20),
        name="step",
    )(snapshots, sketches)
    return turned.T, snapshots - removed


def solution(mesh):
    placed = (P("row", "tm"), P())
    return jax.shard_map(
        body, mesh=mesh, in_specs=placed, out_specs=(P(None, "tm"), P("row", "tm")), check_vma=False
    )
```

```python
import jax
import jax.numpy as jnp
from jax import lax
from jax.experimental import pallas as pl
from jax.experimental.pallas import tpu as pltpu
from jax.sharding import PartitionSpec as P

BF, F32 = jnp.bfloat16, jnp.float32
MESH = pl.DeviceIdType.MESH
NX, NC, NY, NZ = 4, 2, 8, 8
N = 128
ROWS = 1024
SPLIT = 384


def split(a):
    high = a.astype(BF)
    return high, (a - high.astype(F32)).astype(BF)


def mm(a, b):
    ah, al = split(a)
    bh, bl = split(b)
    left = jnp.concatenate([ah, ah, al], 1)
    right = jnp.concatenate([bh, bl, bh], 0)
    return jnp.dot(left, right, preferred_element_type=F32)


def identity():
    down = lax.broadcasted_iota(jnp.int32, (N, N), 0)
    across = lax.broadcasted_iota(jnp.int32, (N, N), 1)
    return jnp.where(down == across, 1.0, 0.0).astype(F32)


def inverse_roots(grams, want_image=True):
    one = identity()
    scales = [jnp.sqrt(jnp.sum(a * a, keepdims=True) + 1e-06) for a in grams]
    ts = [a / s for a, s in zip(grams, scales)]
    zs = ms = [1.5 * one - 0.5 * t for t in ts]
    ts = [mm(mm(t, m), m) for t, m in zip(ts, ms)]
    for step in range(1, 5):
        ms = [1.5 * one - 0.5 * t for t in ts]
        if step == 4 and not want_image:
            zs = [mm(z, m) for z, m in zip(zs, ms)]
        else:
            both = [mm(m, jnp.concatenate([t, z], 1)) for t, z, m in zip(ts, zs, ms)]
            zs = [b[:, N:] for b in both]
            ts = [mm(b[:, :N], m) for b, m in zip(both, ms)]
    return [z / jnp.sqrt(s) for z, s in zip(zs, scales)], ts


def sketched(t_p, t_g, cross, sketch):
    top = jnp.concatenate([t_p, cross.T], 1)
    bottom = jnp.concatenate([cross, t_g], 1)
    gram = jnp.concatenate([top, bottom], 0)
    s = mm(gram, sketch)
    return s, mm(s.T, mm(gram, s))


def tree(root, image, block, own, sketch, halves, gate):
    gate(0)
    r = [root(o) for o in range(8)]
    s0, a0, e0 = [], [], []
    for j in range(4):
        cross = mm(mm(r[2 * j], block(2 * j, 2 * j + 1)), r[2 * j + 1])
        s, a = sketched(image(2 * j + 1), image(2 * j), cross, sketch(0))
        s0.append(s)
        a0.append(a)
    for j in range(4):
        e0.append(jnp.concatenate([mm(r[2 * j + 1], s0[j][:N]), mm(r[2 * j], s0[j][N:])], 0))
    r1, t1 = inverse_roots(a0)
    gate(1)
    gate(2)
    cross1 = []
    for j in range(0, 4, 2):
        upper = jnp.concatenate([block(2 * j + 1, 2 * j + 3), block(2 * j + 1, 2 * j + 2)], 1)
        lower = jnp.concatenate([block(2 * j, 2 * j + 3), block(2 * j, 2 * j + 2)], 1)
        cross1.append(mm(e0[j].T, mm(jnp.concatenate([upper, lower], 0), e0[j + 1])))
    s1, a1, e1 = [], [], []
    for j in range(2):
        cross = mm(mm(r1[2 * j], cross1[j]), r1[2 * j + 1])
        s, a = sketched(t1[2 * j + 1], t1[2 * j], cross, sketch(1))
        s1.append(s)
        a1.append(a)
    for j in range(2):
        upper = mm(e0[2 * j + 1], mm(r1[2 * j + 1], s1[j][:N]))
        lower = mm(e0[2 * j], mm(r1[2 * j], s1[j][N:]))
        e1.append(jnp.concatenate([upper, lower], 0))
    r2, t2 = inverse_roots(a1)
    gate(3)
    wide = [jnp.concatenate([block(a, b) for b in (7, 6, 5, 4)], 1) for a in (3, 2, 1, 0)]
    cross2 = mm(e1[0].T, mm(jnp.concatenate(wide, 0), e1[1]))
    near = jnp.concatenate([block(0, 3), block(0, 2), block(0, 1), own], 1)
    far = jnp.concatenate([block(0, 7), block(0, 6), block(0, 5), block(0, 4)], 1)
    w_far, w_near = mm(far, e1[1]), mm(near, e1[0])
    s2, a2 = sketched(t2[1], t2[0], mm(mm(r2[0], cross2), r2[1]), sketch(2))
    h = mm(jnp.concatenate([mm(w_far, r2[1]), mm(w_near, r2[0])], 1), s2)
    upper = mm(e1[1], mm(r2[1], s2[:N]))
    lower = mm(e1[0], mm(r2[0], s2[N:]))
    high, low = halves()
    mix_h, mix_l = split(jnp.concatenate([upper, lower], 0))
    wide = jnp.concatenate([high, high, low], 1)
    base = jnp.dot(wide, jnp.concatenate([mix_h, mix_l, mix_h], 0), preferred_element_type=F32)
    r3 = inverse_roots([a2], False)[0][0]
    turned = mm(h, r3)
    return turned, mm(base, mm(r3, turned.T))


def place():
    tm, row = lax.axis_index("tm"), lax.axis_index("row")
    c = tm % NC
    y, z = row % NY, row // NY
    return tm // NC, c, y + c * (z - y), z + c * (y - z)


def device(x, c, core, u, v):
    y, z = u + core * (v - u), v + core * (u - v)
    return (x * NC + c, z * NY + y)


def rows_of(index, count):
    return pl.ds(pl.multiple_of(index * count, count), count)


def step(x_hbm, sk_ref, coef_ref, def_ref, x_ref, xall, xh, xl, kall, leaves, roots, part, rsy, rsz, lrow, lsy, lsz,
         g_s, g_r, c_s, c_r, y_s, y_r, z_s, z_r, p1_s, p1_r, p3_s, p3_r, p4_s, p4_r,
         ly_s, ly_r, lz_s, lz_r, b1_s, b1_r, b2_s, b2_r, b4_s, b4_r, load_s):
    x, c, u, v = place()
    tm = x * NC + c
    left, right, across = (x + 3) % NX, (x + 1) % NX, (x + 2) % NX
    peers_x = [device((x + k) % NX, c, c, u, v) for k in range(1, NX)]
    peers_y = [device(x, c, c, (u + k) % NY, v) for k in range(1, NY)]
    peers_z = [device(x, c, c, u, (v + k) % NZ) for k in range(1, NZ)]
    partner = device(x, 1 - c, c, u, v)

    barrier = pltpu.get_barrier_semaphore()
    everyone = peers_x + peers_y + peers_z + [partner]
    for peer in everyone:
        pl.semaphore_signal(barrier, inc=1, device_id=peer, device_id_type=MESH)
    load = pltpu.make_async_copy(x_hbm, x_ref, load_s)
    load.start()
    load.wait()

    mine = x_ref[...]
    xall[x, c] = mine
    mine_h, mine_l = split(mine)
    xh[0] = mine_h
    xl[0] = mine_l
    turned_h, turned_l = split(mine.T)
    turned = jnp.concatenate([turned_h, turned_h, turned_l], 1)

    def gram_with(high, low):
        return jnp.dot(turned, jnp.concatenate([high, low, high], 0), preferred_element_type=F32)

    lrow[...] = gram_with(mine_h, mine_l).reshape(2, 64, N)
    pl.semaphore_wait(barrier, len(everyone))

    def send(src, dst, s, r, peer):
        copy = pltpu.make_async_remote_copy(
            src_ref=src, dst_ref=dst, send_sem=s, recv_sem=r, device_id=peer, device_id_type=MESH
        )
        copy.start()
        return copy

    pending = []
    first, last = pl.ds(0, SPLIT), pl.ds(SPLIT, ROWS - SPLIT)
    to_right, to_left = device(right, c, c, u, v), device(left, c, c, u, v)

    def hop(k, source, part_of, peer, src=None):
        src = xall.at[source, c, part_of] if src is None else src
        copy = send(src, xall.at[source, c, part_of], g_s.at[k], g_r.at[k], peer)
        pending.append(copy)
        return copy

    def passed(k, source, part_of):
        here = xall.at[source, c, part_of]
        copy = send(here, here, c_s.at[k], c_r.at[k], partner)
        pending.append(copy)
        return copy

    hop0 = hop(0, x, first, to_right, x_ref.at[first])
    hop1 = hop(1, x, last, to_left, x_ref.at[last])
    hop2 = hop(2, x, last, to_right, x_ref.at[last])
    whole = send(x_ref, xall.at[x, c], c_s.at[6], c_r.at[6], partner)
    pending.append(whole)
    copies = [
        send(lrow.at[:, rows_of((u + k) % NY, 8), :], lsy.at[k - 1], ly_s.at[k - 1], ly_r.at[k - 1], peers_y[k - 1])
        for k in range(1, NY)
    ]
    total = lrow[:, rows_of(u, 8), :]
    for k, copy in enumerate(copies):
        copy.wait_recv()
        total += lsy[k]
    pending += copies
    lsz[NZ - 1] = total
    copies = [
        send(lsz.at[NZ - 1], lsz.at[k - 1], lz_s.at[k - 1], lz_r.at[k - 1], peers_z[k - 1])
        for k in range(1, NZ)
    ]

    hop0.wait_recv()
    hop4 = hop(4, left, first, to_right)
    chip0 = passed(0, left, first)

    def in_order(slots):
        total = slots[(v + NZ - 1) % NZ]
        for source in range(1, NZ):
            total += slots[(v - source + NZ - 1) % NZ]
        return total

    def received(copies):
        for copy in copies:
            copy.wait_recv()
        pending.extend(copies)

    spot = rows_of(u, 8)

    def at(o):
        g = (tm - o + 8) % 8
        return g // NC, g % NC

    def to_line(src, dst, s, r, peers):
        return [send(src, dst, s.at[k], r.at[k], peer) for k, peer in enumerate(peers)]

    def same(ref, s, r, peers):
        return to_line(ref, ref, s, r, peers)

    received(copies)
    leaves[c, :, x, spot, :] = in_order(lsz)
    leaf_x = same(leaves.at[c, :, x, spot, :], b1_s, b1_r, peers_x)
    hop1.wait_recv()
    hop5 = hop(5, right, last, to_left)
    hop3 = hop(3, x, first, to_left, x_ref.at[first])
    chip1 = passed(1, right, last)
    hop2.wait_recv()
    chip2 = passed(2, left, last)

    def prepare(o):
        gx, gc = at(o)
        high, low = split(xall[gx, gc])
        xh[o] = high
        xl[o] = low
        return high, low

    def cross_gram(d):
        part[d - 1] = gram_with(*prepare(d)).reshape(2, 64, N)

    def scatter(half):
        pair = pl.ds(2 * half, 2)
        return [
            send(
                part.at[pair, :, rows_of((u + k) % NY, 8), :],
                rsy.at[half, k - 1],
                y_s.at[half, k - 1],
                y_r.at[half, k - 1],
                peers_y[k - 1],
            )
            for k in range(1, NY)
        ]

    def spread(half, copies):
        received(copies)
        total = part[2 * half : 2 * half + 2, :, spot, :]
        for k in range(NY - 1):
            total += rsy[half, k]
        rsz[half, NZ - 1] = total.reshape(4, 8, N)
        return [
            send(rsz.at[half, NZ - 1], rsz.at[half, k], z_s.at[half, k], z_r.at[half, k], peers_z[k])
            for k in range(NZ - 1)
        ]

    def along_x(half, copies):
        received(copies)
        quad = pl.ds(4 * half, 4)
        kall[c, quad, x, spot, :] = in_order(rsz.at[half])
        return same(kall.at[c, quad, x, spot, :], p1_s.at[half], p1_r.at[half], peers_x)

    def along_u(half, copies):
        received(copies)
        return [
            same(kall.at[c, pl.ds(2 * d, 2), :, spot, :], p3_s.at[d], p3_r.at[d], peers_y)
            for d in (2 * half, 2 * half + 1)
        ]

    def swap(d, copies):
        received(copies)
        pair = pl.ds(2 * d, 2)
        over = send(kall.at[c, pair], kall.at[c, pair], p4_s.at[d], p4_r.at[d], partner)
        pending.append(over)
        return over

    whole.wait_recv()
    chip0.wait_recv()
    chip2.wait_recv()
    cross_gram(1)
    cross_gram(2)
    near = scatter(0)
    hop4.wait_recv()
    chip4 = passed(4, across, first)
    hop5.wait_recv()
    chip5 = passed(5, across, last)
    near = spread(0, near)
    received(leaf_x)
    leaf_u = same(leaves.at[c, :, :, spot, :], b2_s, b2_r, peers_y)
    chip4.wait_recv()
    chip5.wait_recv()
    cross_gram(3)
    cross_gram(4)
    far = scatter(1)
    hop3.wait_recv()
    chip3 = passed(3, right, first)
    near = along_x(0, near)
    far = spread(1, far)
    received(leaf_u)
    over = send(leaves.at[c], leaves.at[c], b4_s, b4_r, partner)
    pending.append(over)
    near = along_u(0, near)
    over.wait_recv()

    def leaf(o):
        gx, gc = at(o)
        return jnp.concatenate([leaves[gc, 0, gx], leaves[gc, 1, gx]], 0)

    def leaf_roots(first_o):
        some, images = inverse_roots([leaf(first_o + i) for i in range(4)])
        for i in range(4):
            roots[first_o + i] = some[i]
            roots[8 + first_o + i] = images[i]

    leaf_roots(0)
    far = along_x(1, far)
    leaf_roots(4)
    overs = [swap(0, near[0])]
    far = along_u(1, far)
    chip1.wait_recv()
    chip3.wait_recv()
    for o in (5, 6, 7):
        prepare(o)

    def gate(d):
        if d == 1:
            overs.append(swap(1, near[1]))
        if d == 2:
            overs.append(swap(2, far[0]))
        if d == 3:
            overs.append(swap(3, far[1]))
        overs[d].wait_recv()

    def stored(o, d):
        gx, gc = at(o)
        return jnp.concatenate([kall[gc, 2 * d - 2, gx], kall[gc, 2 * d - 1, gx]], 0)

    def block(a, b):
        return stored(a, b - a) if b - a <= 4 else stored(b, 8 - b + a).T

    def halves():
        return [jnp.concatenate([ref[o] for o in range(7, -1, -1)], 1) for ref in (xh, xl)]

    coef_ref[...], def_ref[...] = tree(
        lambda o: roots[o],
        lambda o: roots[8 + o],
        block,
        leaf(0),
        lambda level: sk_ref[level],
        halves,
        gate,
    )
    for copy in pending:
        copy.wait_send()


def outputs(x_ref, removed_ref, turned_ref, coefficients_ref, deflated_ref):
    coefficients_ref[...] = turned_ref[...].T
    deflated_ref[...] = x_ref[...] - removed_ref[...]


def body(snapshots, sketches):
    dma = pltpu.SemaphoreType.DMA
    vmem = pl.BlockSpec(memory_space=pltpu.VMEM)
    counts = [6, 6, 7, 7, (2, 7), (2, 7), (2, 7), (2, 7), (2, 3), (2, 3), (4, 7), (4, 7), 4, 4, 7, 7, 7, 7, 3, 3, 7, 7]
    shapes = [
        (NC, NZ, NX, 64, N),
        (NC, 2, NX, 64, N),
        (16, N, N),
        (4, 2, 64, N),
        (2, NY - 1, 2, 2, 8, N),
        (2, NZ, 4, 8, N),
        (2, 64, N),
        (NY - 1, 2, 8, N),
        (NZ, 2, 8, N),
    ]
    turned, removed = pl.pallas_call(
        step,
        out_shape=[jax.ShapeDtypeStruct((N, N), F32), jax.ShapeDtypeStruct((ROWS, N), F32)],
        in_specs=[pl.BlockSpec(memory_space=pl.ANY), vmem],
        out_specs=[vmem] * 2,
        scratch_shapes=[
            pltpu.VMEM((ROWS, N), F32),
            pltpu.VMEM((NX, NC, ROWS, N), F32),
            pltpu.VMEM((2 * NX, ROWS, N), BF),
            pltpu.VMEM((2 * NX, ROWS, N), BF),
            *[pltpu.VMEM(s, F32) for s in shapes],
            *[dma(n if isinstance(n, tuple) else (n,)) for n in counts],
            dma,
            dma,
            dma,
        ],
        compiler_params=pltpu.CompilerParams(collective_id=0, has_side_effects=True, vmem_limit_bytes=60 << 20),
        name="step",
    )(snapshots, sketches)
    return pl.pallas_call(
        outputs,
        out_shape=[jax.ShapeDtypeStruct((N, N), F32), jax.ShapeDtypeStruct((ROWS, N), F32)],
        in_specs=[vmem] * 3,
        out_specs=[vmem] * 2,
        name="outputs",
    )(snapshots, removed, turned)


def solution(mesh):
    placed = (P("row", "tm"), P())
    return jax.shard_map(
        body, mesh=mesh, in_specs=placed, out_specs=(P(None, "tm"), P("row", "tm")), check_vma=False
    )
```

```python
import jax
import jax.numpy as jnp
from jax import lax
from jax.experimental import pallas as pl
from jax.experimental.pallas import tpu as pltpu
from jax.sharding import PartitionSpec as P

BF, F32 = jnp.bfloat16, jnp.float32
MESH = pl.DeviceIdType.MESH
NX, NC, NY, NZ = 4, 2, 8, 8
N = 128
ROWS = 1024
SPLIT = 384


def split(a):
    high = a.astype(BF)
    return high, (a - high.astype(F32)).astype(BF)


def mm(a, b):
    ah, al = split(a)
    bh, bl = split(b)
    left = jnp.concatenate([ah, ah, al], 1)
    right = jnp.concatenate([bh, bl, bh], 0)
    return jnp.dot(left, right, preferred_element_type=F32)


def identity():
    down = lax.broadcasted_iota(jnp.int32, (N, N), 0)
    across = lax.broadcasted_iota(jnp.int32, (N, N), 1)
    return jnp.where(down == across, 1.0, 0.0).astype(F32)


def inverse_roots(grams, want_image=True):
    one = identity()
    scales = [jnp.sqrt(jnp.sum(a * a, keepdims=True) + 1e-06) for a in grams]
    ts = [a / s for a, s in zip(grams, scales)]
    zs = ms = [1.5 * one - 0.5 * t for t in ts]
    ts = [mm(mm(t, m), m) for t, m in zip(ts, ms)]
    for step in range(1, 5):
        ms = [1.5 * one - 0.5 * t for t in ts]
        if step == 4 and not want_image:
            zs = [mm(z, m) for z, m in zip(zs, ms)]
        else:
            both = [mm(m, jnp.concatenate([t, z], 1)) for t, z, m in zip(ts, zs, ms)]
            zs = [b[:, N:] for b in both]
            ts = [mm(b[:, :N], m) for b, m in zip(both, ms)]
    return [z / jnp.sqrt(s) for z, s in zip(zs, scales)], ts


def sketched(t_p, t_g, cross, sketch):
    top = jnp.concatenate([t_p, cross.T], 1)
    bottom = jnp.concatenate([cross, t_g], 1)
    gram = jnp.concatenate([top, bottom], 0)
    s = mm(gram, sketch)
    return s, mm(s.T, mm(gram, s))


def tree(root, image, block, own, sketch, halves, gate):
    gate(0)
    r = [root(o) for o in range(8)]
    s0, a0, e0 = [], [], []
    for j in range(4):
        cross = mm(mm(r[2 * j], block(2 * j, 2 * j + 1)), r[2 * j + 1])
        s, a = sketched(image(2 * j + 1), image(2 * j), cross, sketch(0))
        s0.append(s)
        a0.append(a)
    for j in range(4):
        e0.append(jnp.concatenate([mm(r[2 * j + 1], s0[j][:N]), mm(r[2 * j], s0[j][N:])], 0))
    r1, t1 = inverse_roots(a0)
    gate(1)
    gate(2)
    cross1 = []
    for j in range(0, 4, 2):
        upper = jnp.concatenate([block(2 * j + 1, 2 * j + 3), block(2 * j + 1, 2 * j + 2)], 1)
        lower = jnp.concatenate([block(2 * j, 2 * j + 3), block(2 * j, 2 * j + 2)], 1)
        cross1.append(mm(e0[j].T, mm(jnp.concatenate([upper, lower], 0), e0[j + 1])))
    s1, a1, e1 = [], [], []
    for j in range(2):
        cross = mm(mm(r1[2 * j], cross1[j]), r1[2 * j + 1])
        s, a = sketched(t1[2 * j + 1], t1[2 * j], cross, sketch(1))
        s1.append(s)
        a1.append(a)
    for j in range(2):
        upper = mm(e0[2 * j + 1], mm(r1[2 * j + 1], s1[j][:N]))
        lower = mm(e0[2 * j], mm(r1[2 * j], s1[j][N:]))
        e1.append(jnp.concatenate([upper, lower], 0))
    r2, t2 = inverse_roots(a1)
    gate(3)
    wide = [jnp.concatenate([block(a, b) for b in (7, 6, 5, 4)], 1) for a in (3, 2, 1, 0)]
    cross2 = mm(e1[0].T, mm(jnp.concatenate(wide, 0), e1[1]))
    near = jnp.concatenate([block(0, 3), block(0, 2), block(0, 1), own], 1)
    far = jnp.concatenate([block(0, 7), block(0, 6), block(0, 5), block(0, 4)], 1)
    w_far, w_near = mm(far, e1[1]), mm(near, e1[0])
    s2, a2 = sketched(t2[1], t2[0], mm(mm(r2[0], cross2), r2[1]), sketch(2))
    h = mm(jnp.concatenate([mm(w_far, r2[1]), mm(w_near, r2[0])], 1), s2)
    upper = mm(e1[1], mm(r2[1], s2[:N]))
    lower = mm(e1[0], mm(r2[0], s2[N:]))
    high, low = halves()
    mix_h, mix_l = split(jnp.concatenate([upper, lower], 0))
    wide = jnp.concatenate([high, high, low], 1)
    base = jnp.dot(wide, jnp.concatenate([mix_h, mix_l, mix_h], 0), preferred_element_type=F32)
    r3 = inverse_roots([a2], False)[0][0]
    turned = mm(h, r3)
    return turned, mm(base, mm(r3, turned.T))


def place():
    tm, row = lax.axis_index("tm"), lax.axis_index("row")
    c = tm % NC
    y, z = row % NY, row // NY
    return tm // NC, c, y + c * (z - y), z + c * (y - z)


def device(x, c, core, u, v):
    y, z = u + core * (v - u), v + core * (u - v)
    return (x * NC + c, z * NY + y)


def rows_of(index, count):
    return pl.ds(pl.multiple_of(index * count, count), count)


def step(x_hbm, sk_ref, coef_ref, def_ref, x_ref, xall, xh, xl, kall, leaves, roots, part, rsy, rsz, lrow, lsy, lsz,
         g_s, g_r, c_s, c_r, y_s, y_r, z_s, z_r, p1_s, p1_r, p3_s, p3_r, p4_s, p4_r,
         ly_s, ly_r, lz_s, lz_r, b1_s, b1_r, b2_s, b2_r, b4_s, b4_r, load_s):
    x, c, u, v = place()
    tm = x * NC + c
    left, right, across = (x + 3) % NX, (x + 1) % NX, (x + 2) % NX
    peers_x = [device((x + k) % NX, c, c, u, v) for k in range(1, NX)]
    peers_y = [device(x, c, c, (u + k) % NY, v) for k in range(1, NY)]
    peers_z = [device(x, c, c, u, (v + k) % NZ) for k in range(1, NZ)]
    partner = device(x, 1 - c, c, u, v)

    barrier = pltpu.get_barrier_semaphore()
    everyone = peers_x + peers_y + peers_z + [partner]
    for peer in everyone:
        pl.semaphore_signal(barrier, inc=1, device_id=peer, device_id_type=MESH)
    load = pltpu.make_async_copy(x_hbm, x_ref, load_s)
    load.start()
    load.wait()

    mine = x_ref[...]
    xall[x, c] = mine
    mine_h, mine_l = split(mine)
    xh[0] = mine_h
    xl[0] = mine_l
    turned_h, turned_l = split(mine.T)
    turned = jnp.concatenate([turned_h, turned_h, turned_l], 1)

    def gram_with(high, low):
        return jnp.dot(turned, jnp.concatenate([high, low, high], 0), preferred_element_type=F32)

    lrow[...] = gram_with(mine_h, mine_l).reshape(2, 64, N)
    pl.semaphore_wait(barrier, len(everyone))

    def send(src, dst, s, r, peer):
        copy = pltpu.make_async_remote_copy(
            src_ref=src, dst_ref=dst, send_sem=s, recv_sem=r, device_id=peer, device_id_type=MESH
        )
        copy.start()
        return copy

    pending = []
    first, last = pl.ds(0, SPLIT), pl.ds(SPLIT, ROWS - SPLIT)
    to_right, to_left = device(right, c, c, u, v), device(left, c, c, u, v)

    def hop(k, source, part_of, peer, src=None):
        src = xall.at[source, c, part_of] if src is None else src
        copy = send(src, xall.at[source, c, part_of], g_s.at[k], g_r.at[k], peer)
        pending.append(copy)
        return copy

    def passed(k, source, part_of):
        here = xall.at[source, c, part_of]
        copy = send(here, here, c_s.at[k], c_r.at[k], partner)
        pending.append(copy)
        return copy

    hop0 = hop(0, x, first, to_right, x_ref.at[first])
    hop1 = hop(1, x, last, to_left, x_ref.at[last])
    hop2 = hop(2, x, last, to_right, x_ref.at[last])
    whole = send(x_ref, xall.at[x, c], c_s.at[6], c_r.at[6], partner)
    pending.append(whole)
    copies = [
        send(lrow.at[:, rows_of((u + k) % NY, 8), :], lsy.at[k - 1], ly_s.at[k - 1], ly_r.at[k - 1], peers_y[k - 1])
        for k in range(1, NY)
    ]
    total = lrow[:, rows_of(u, 8), :]
    for k, copy in enumerate(copies):
        copy.wait_recv()
        total += lsy[k]
    pending += copies
    lsz[NZ - 1] = total
    copies = [
        send(lsz.at[NZ - 1], lsz.at[k - 1], lz_s.at[k - 1], lz_r.at[k - 1], peers_z[k - 1])
        for k in range(1, NZ)
    ]

    hop0.wait_recv()
    hop4 = hop(4, left, first, to_right)
    chip0 = passed(0, left, first)

    def in_order(slots):
        total = slots[(v + NZ - 1) % NZ]
        for source in range(1, NZ):
            total += slots[(v - source + NZ - 1) % NZ]
        return total

    def received(copies):
        for copy in copies:
            copy.wait_recv()
        pending.extend(copies)

    spot = rows_of(u, 8)

    def at(o):
        g = (tm - o + 8) % 8
        return g // NC, g % NC

    def to_line(src, dst, s, r, peers):
        return [send(src, dst, s.at[k], r.at[k], peer) for k, peer in enumerate(peers)]

    def same(ref, s, r, peers):
        return to_line(ref, ref, s, r, peers)

    received(copies)
    leaves[c, :, x, spot, :] = in_order(lsz)
    leaf_u = same(leaves.at[c, :, x, spot, :], b2_s, b2_r, peers_y)
    hop1.wait_recv()
    hop5 = hop(5, right, last, to_left)
    chip1 = passed(1, right, last)
    hop2.wait_recv()
    chip2 = passed(2, left, last)

    def prepare(o):
        gx, gc = at(o)
        high, low = split(xall[gx, gc])
        xh[o] = high
        xl[o] = low
        return high, low

    def cross_gram(d):
        part[d - 1] = gram_with(*prepare(d)).reshape(2, 64, N)

    def scatter(half):
        pair = pl.ds(2 * half, 2)
        return [
            send(
                part.at[pair, :, rows_of((u + k) % NY, 8), :],
                rsy.at[half, k - 1],
                y_s.at[half, k - 1],
                y_r.at[half, k - 1],
                peers_y[k - 1],
            )
            for k in range(1, NY)
        ]

    def spread(half, copies):
        received(copies)
        total = part[2 * half : 2 * half + 2, :, spot, :]
        for k in range(NY - 1):
            total += rsy[half, k]
        rsz[half, NZ - 1] = total.reshape(4, 8, N)
        return [
            send(rsz.at[half, NZ - 1], rsz.at[half, k], z_s.at[half, k], z_r.at[half, k], peers_z[k])
            for k in range(NZ - 1)
        ]

    def own_rows(half, copies):
        received(copies)
        quad = pl.ds(4 * half, 4)
        kall[c, quad, x, spot, :] = in_order(rsz.at[half])
        return kall.at[c, quad, x, spot, :]

    def along_x(half, copies):
        return same(own_rows(half, copies), p1_s.at[0], p1_r.at[0], peers_x)

    def along_u(half, copies):
        received(copies)
        return [
            same(kall.at[c, pl.ds(2 * d, 2), :, spot, :], p3_s.at[d], p3_r.at[d], peers_y)
            for d in (2 * half, 2 * half + 1)
        ]

    def own_along_u(copies):
        return same(own_rows(1, copies), p3_s.at[2], p3_r.at[2], peers_y)

    def whole_along_x(copies):
        received(copies)
        return [same(kall.at[c, pl.ds(2 * d, 2), x], p1_s.at[d - 1], p1_r.at[d - 1], peers_x) for d in (2, 3)]

    def swap(d, copies):
        received(copies)
        pair = pl.ds(2 * d, 2)
        over = send(kall.at[c, pair], kall.at[c, pair], p4_s.at[d], p4_r.at[d], partner)
        pending.append(over)
        return over

    whole.wait_recv()
    chip0.wait_recv()
    chip2.wait_recv()
    cross_gram(1)
    cross_gram(2)
    near = scatter(0)
    received(leaf_u)
    leaf_x = same(leaves.at[c, :, x], b1_s, b1_r, peers_x)
    hop3 = hop(3, x, first, to_left, x_ref.at[first])
    hop4.wait_recv()
    chip4 = passed(4, across, first)
    hop5.wait_recv()
    chip5 = passed(5, across, last)
    near = spread(0, near)
    chip4.wait_recv()
    chip5.wait_recv()
    cross_gram(3)
    cross_gram(4)
    far = scatter(1)
    received(leaf_x)
    over = send(leaves.at[c], leaves.at[c], b4_s, b4_r, partner)
    pending.append(over)
    near = along_x(0, near)
    far = spread(1, far)
    over.wait_recv()

    def leaf(o):
        gx, gc = at(o)
        return jnp.concatenate([leaves[gc, 0, gx], leaves[gc, 1, gx]], 0)

    def leaf_roots(first_o):
        some, images = inverse_roots([leaf(first_o + i) for i in range(4)])
        for i in range(4):
            roots[first_o + i] = some[i]
            roots[8 + first_o + i] = images[i]

    leaf_roots(0)
    near = along_u(0, near)
    leaf_roots(4)
    far = own_along_u(far)
    hop3.wait_recv()
    chip3 = passed(3, right, first)
    chip1.wait_recv()
    chip3.wait_recv()
    for o in (5, 6, 7):
        prepare(o)
    overs = [swap(0, near[0])]
    far = whole_along_x(far)

    def gate(d):
        if d == 1:
            overs.append(swap(1, near[1]))
        if d == 2:
            overs.append(swap(2, far[0]))
        if d == 3:
            overs.append(swap(3, far[1]))
        overs[d].wait_recv()

    def stored(o, d):
        gx, gc = at(o)
        return jnp.concatenate([kall[gc, 2 * d - 2, gx], kall[gc, 2 * d - 1, gx]], 0)

    def block(a, b):
        return stored(a, b - a) if b - a <= 4 else stored(b, 8 - b + a).T

    def halves():
        return [jnp.concatenate([ref[o] for o in range(7, -1, -1)], 1) for ref in (xh, xl)]

    coef_ref[...], def_ref[...] = tree(
        lambda o: roots[o],
        lambda o: roots[8 + o],
        block,
        leaf(0),
        lambda level: sk_ref[level],
        halves,
        gate,
    )
    for copy in pending:
        copy.wait_send()


def outputs(x_ref, removed_ref, turned_ref, coefficients_ref, deflated_ref):
    coefficients_ref[...] = turned_ref[...].T
    deflated_ref[...] = x_ref[...] - removed_ref[...]


def body(snapshots, sketches):
    dma = pltpu.SemaphoreType.DMA
    vmem = pl.BlockSpec(memory_space=pltpu.VMEM)
    counts = [6, 6, 7, 7, (2, 7), (2, 7), (2, 7), (2, 7), (3, 3), (3, 3), (3, 7), (3, 7), 4, 4, 7, 7, 7, 7, 3, 3, 7, 7]
    shapes = [
        (NC, NZ, NX, 64, N),
        (NC, 2, NX, 64, N),
        (16, N, N),
        (4, 2, 64, N),
        (2, NY - 1, 2, 2, 8, N),
        (2, NZ, 4, 8, N),
        (2, 64, N),
        (NY - 1, 2, 8, N),
        (NZ, 2, 8, N),
    ]
    turned, removed = pl.pallas_call(
        step,
        out_shape=[jax.ShapeDtypeStruct((N, N), F32), jax.ShapeDtypeStruct((ROWS, N), F32)],
        in_specs=[pl.BlockSpec(memory_space=pl.ANY), vmem],
        out_specs=[vmem] * 2,
        scratch_shapes=[
            pltpu.VMEM((ROWS, N), F32),
            pltpu.VMEM((NX, NC, ROWS, N), F32),
            pltpu.VMEM((2 * NX, ROWS, N), BF),
            pltpu.VMEM((2 * NX, ROWS, N), BF),
            *[pltpu.VMEM(s, F32) for s in shapes],
            *[dma(n if isinstance(n, tuple) else (n,)) for n in counts],
            dma,
            dma,
            dma,
        ],
        compiler_params=pltpu.CompilerParams(collective_id=0, has_side_effects=True, vmem_limit_bytes=60 << 20),
        name="step",
    )(snapshots, sketches)
    return pl.pallas_call(
        outputs,
        out_shape=[jax.ShapeDtypeStruct((N, N), F32), jax.ShapeDtypeStruct((ROWS, N), F32)],
        in_specs=[vmem] * 3,
        out_specs=[vmem] * 2,
        name="outputs",
    )(snapshots, removed, turned)


def solution(mesh):
    placed = (P("row", "tm"), P())
    return jax.shard_map(
        body, mesh=mesh, in_specs=placed, out_specs=(P(None, "tm"), P("row", "tm")), check_vma=False
    )
```

```python
import jax
import jax.numpy as jnp
from jax import lax
from jax.experimental import pallas as pl
from jax.experimental.pallas import tpu as pltpu
from jax.sharding import PartitionSpec as P

BF, F32 = jnp.bfloat16, jnp.float32
MESH = pl.DeviceIdType.MESH
NX, NC, NY, NZ = 4, 2, 8, 8
N = 128
ROWS = 1024
SPLIT = 384


def split(a):
    high = a.astype(BF)
    return high, (a - high.astype(F32)).astype(BF)


def mm(a, b):
    ah, al = split(a)
    bh, bl = split(b)
    left = jnp.concatenate([ah, ah, al], 1)
    right = jnp.concatenate([bh, bl, bh], 0)
    return jnp.dot(left, right, preferred_element_type=F32)


def identity():
    down = lax.broadcasted_iota(jnp.int32, (N, N), 0)
    across = lax.broadcasted_iota(jnp.int32, (N, N), 1)
    return jnp.where(down == across, 1.0, 0.0).astype(F32)


def inverse_roots(grams, want_image=True):
    one = identity()
    scales = [jnp.sqrt(jnp.sum(a * a, keepdims=True) + 1e-06) for a in grams]
    ts = [a / s for a, s in zip(grams, scales)]
    zs = ms = [1.5 * one - 0.5 * t for t in ts]
    ts = [mm(mm(t, m), m) for t, m in zip(ts, ms)]
    for step in range(1, 5):
        ms = [1.5 * one - 0.5 * t for t in ts]
        if step == 4 and not want_image:
            zs = [mm(z, m) for z, m in zip(zs, ms)]
        else:
            both = [mm(m, jnp.concatenate([t, z], 1)) for t, z, m in zip(ts, zs, ms)]
            zs = [b[:, N:] for b in both]
            ts = [mm(b[:, :N], m) for b, m in zip(both, ms)]
    return [z / jnp.sqrt(s) for z, s in zip(zs, scales)], ts


def sketched(t_p, t_g, cross, sketch):
    top = jnp.concatenate([t_p, cross.T], 1)
    bottom = jnp.concatenate([cross, t_g], 1)
    gram = jnp.concatenate([top, bottom], 0)
    s = mm(gram, sketch)
    return s, mm(s.T, mm(gram, s))


def tree(root, image, block, own, sketch, halves, gate):
    gate(0)
    r = [root(o) for o in range(8)]
    s0, a0, e0 = [], [], []
    for j in range(4):
        cross = mm(mm(r[2 * j], block(2 * j, 2 * j + 1)), r[2 * j + 1])
        s, a = sketched(image(2 * j + 1), image(2 * j), cross, sketch(0))
        s0.append(s)
        a0.append(a)
    for j in range(4):
        e0.append(jnp.concatenate([mm(r[2 * j + 1], s0[j][:N]), mm(r[2 * j], s0[j][N:])], 0))
    gate(1)
    r1, t1 = inverse_roots(a0)
    gate(2)
    cross1 = []
    for j in range(0, 4, 2):
        upper = jnp.concatenate([block(2 * j + 1, 2 * j + 3), block(2 * j + 1, 2 * j + 2)], 1)
        lower = jnp.concatenate([block(2 * j, 2 * j + 3), block(2 * j, 2 * j + 2)], 1)
        cross1.append(mm(e0[j].T, mm(jnp.concatenate([upper, lower], 0), e0[j + 1])))
    s1, a1, e1 = [], [], []
    for j in range(2):
        cross = mm(mm(r1[2 * j], cross1[j]), r1[2 * j + 1])
        s, a = sketched(t1[2 * j + 1], t1[2 * j], cross, sketch(1))
        s1.append(s)
        a1.append(a)
    for j in range(2):
        upper = mm(e0[2 * j + 1], mm(r1[2 * j + 1], s1[j][:N]))
        lower = mm(e0[2 * j], mm(r1[2 * j], s1[j][N:]))
        e1.append(jnp.concatenate([upper, lower], 0))
    r2, t2 = inverse_roots(a1)
    gate(3)
    wide = [jnp.concatenate([block(a, b) for b in (7, 6, 5, 4)], 1) for a in (3, 2, 1, 0)]
    cross2 = mm(e1[0].T, mm(jnp.concatenate(wide, 0), e1[1]))
    near = jnp.concatenate([block(0, 3), block(0, 2), block(0, 1), own], 1)
    far = jnp.concatenate([block(0, 7), block(0, 6), block(0, 5), block(0, 4)], 1)
    w_far, w_near = mm(far, e1[1]), mm(near, e1[0])
    s2, a2 = sketched(t2[1], t2[0], mm(mm(r2[0], cross2), r2[1]), sketch(2))
    h = mm(jnp.concatenate([mm(w_far, r2[1]), mm(w_near, r2[0])], 1), s2)
    upper = mm(e1[1], mm(r2[1], s2[:N]))
    lower = mm(e1[0], mm(r2[0], s2[N:]))
    high, low = halves()
    mix_h, mix_l = split(jnp.concatenate([upper, lower], 0))
    wide = jnp.concatenate([high, high, low], 1)
    base = jnp.dot(wide, jnp.concatenate([mix_h, mix_l, mix_h], 0), preferred_element_type=F32)
    r3 = inverse_roots([a2], False)[0][0]
    turned = mm(h, r3)
    return turned, mm(base, mm(r3, turned.T))


def place():
    tm, row = lax.axis_index("tm"), lax.axis_index("row")
    c = tm % NC
    y, z = row % NY, row // NY
    return tm // NC, c, y + c * (z - y), z + c * (y - z)


def device(x, c, core, u, v):
    y, z = u + core * (v - u), v + core * (u - v)
    return (x * NC + c, z * NY + y)


def rows_of(index, count):
    return pl.ds(pl.multiple_of(index * count, count), count)


def step(x_hbm, sk_ref, coef_ref, def_ref, x_ref, xall, xh, xl, kall, leaves, roots, part, rsy, rsz, lrow, lsy, lsz,
         g_s, g_r, c_s, c_r, y_s, y_r, z_s, z_r, p1_s, p1_r, p3_s, p3_r, p4_s, p4_r,
         ly_s, ly_r, lz_s, lz_r, b1_s, b1_r, b2_s, b2_r, b4_s, b4_r, load_s):
    x, c, u, v = place()
    tm = x * NC + c
    left, right, across = (x + 3) % NX, (x + 1) % NX, (x + 2) % NX
    peers_x = [device((x + k) % NX, c, c, u, v) for k in range(1, NX)]
    peers_y = [device(x, c, c, (u + k) % NY, v) for k in range(1, NY)]
    peers_z = [device(x, c, c, u, (v + k) % NZ) for k in range(1, NZ)]
    partner = device(x, 1 - c, c, u, v)

    barrier = pltpu.get_barrier_semaphore()
    everyone = peers_x + peers_y + peers_z + [partner]
    for peer in everyone:
        pl.semaphore_signal(barrier, inc=1, device_id=peer, device_id_type=MESH)
    load = pltpu.make_async_copy(x_hbm, x_ref, load_s)
    load.start()
    load.wait()

    mine = x_ref[...]
    xall[x, c] = mine
    mine_h, mine_l = split(mine)
    xh[0] = mine_h
    xl[0] = mine_l
    turned_h, turned_l = split(mine.T)
    turned = jnp.concatenate([turned_h, turned_h, turned_l], 1)

    def gram_with(high, low):
        return jnp.dot(turned, jnp.concatenate([high, low, high], 0), preferred_element_type=F32)

    lrow[...] = gram_with(mine_h, mine_l).reshape(2, 64, N)
    pl.semaphore_wait(barrier, len(everyone))

    def send(src, dst, s, r, peer):
        copy = pltpu.make_async_remote_copy(
            src_ref=src, dst_ref=dst, send_sem=s, recv_sem=r, device_id=peer, device_id_type=MESH
        )
        copy.start()
        return copy

    pending = []
    first, last = pl.ds(0, SPLIT), pl.ds(SPLIT, ROWS - SPLIT)
    to_right, to_left = device(right, c, c, u, v), device(left, c, c, u, v)

    def hop(k, source, part_of, peer, src=None):
        src = xall.at[source, c, part_of] if src is None else src
        copy = send(src, xall.at[source, c, part_of], g_s.at[k], g_r.at[k], peer)
        pending.append(copy)
        return copy

    def passed(k, source, part_of):
        here = xall.at[source, c, part_of]
        copy = send(here, here, c_s.at[k], c_r.at[k], partner)
        pending.append(copy)
        return copy

    hop0 = hop(0, x, first, to_right, x_ref.at[first])
    hop1 = hop(1, x, last, to_left, x_ref.at[last])
    hop2 = hop(2, x, last, to_right, x_ref.at[last])
    whole = send(x_ref, xall.at[x, c], c_s.at[6], c_r.at[6], partner)
    pending.append(whole)
    copies = [
        send(lrow.at[:, rows_of((u + k) % NY, 8), :], lsy.at[k - 1], ly_s.at[k - 1], ly_r.at[k - 1], peers_y[k - 1])
        for k in range(1, NY)
    ]
    total = lrow[:, rows_of(u, 8), :]
    for k, copy in enumerate(copies):
        copy.wait_recv()
        total += lsy[k]
    pending += copies
    lsz[NZ - 1] = total
    copies = [
        send(lsz.at[NZ - 1], lsz.at[k - 1], lz_s.at[k - 1], lz_r.at[k - 1], peers_z[k - 1])
        for k in range(1, NZ)
    ]

    hop0.wait_recv()
    hop4 = hop(4, left, first, to_right)
    chip0 = passed(0, left, first)

    def in_order(slots):
        total = slots[(v + NZ - 1) % NZ]
        for source in range(1, NZ):
            total += slots[(v - source + NZ - 1) % NZ]
        return total

    def received(copies):
        for copy in copies:
            copy.wait_recv()
        pending.extend(copies)

    spot = rows_of(u, 8)

    def at(o):
        g = (tm - o + 8) % 8
        return g // NC, g % NC

    def to_line(src, dst, s, r, peers):
        return [send(src, dst, s.at[k], r.at[k], peer) for k, peer in enumerate(peers)]

    def same(ref, s, r, peers):
        return to_line(ref, ref, s, r, peers)

    received(copies)
    leaves[c, :, x, spot, :] = in_order(lsz)
    leaf_u = same(leaves.at[c, :, x, spot, :], b2_s, b2_r, peers_y)
    hop1.wait_recv()
    hop5 = hop(5, right, last, to_left)
    chip1 = passed(1, right, last)
    hop2.wait_recv()
    chip2 = passed(2, left, last)

    def prepare(o):
        gx, gc = at(o)
        high, low = split(xall[gx, gc])
        xh[o] = high
        xl[o] = low
        return high, low

    def cross_gram(d):
        part[d - 1] = gram_with(*prepare(d)).reshape(2, 64, N)

    def scatter(half):
        pair = pl.ds(2 * half, 2)
        return [
            send(
                part.at[pair, :, rows_of((u + k) % NY, 8), :],
                rsy.at[half, k - 1],
                y_s.at[half, k - 1],
                y_r.at[half, k - 1],
                peers_y[k - 1],
            )
            for k in range(1, NY)
        ]

    def spread(half, copies):
        received(copies)
        total = part[2 * half : 2 * half + 2, :, spot, :]
        for k in range(NY - 1):
            total += rsy[half, k]
        rsz[half, NZ - 1] = total.reshape(4, 8, N)
        return [
            send(rsz.at[half, NZ - 1], rsz.at[half, k], z_s.at[half, k], z_r.at[half, k], peers_z[k])
            for k in range(NZ - 1)
        ]

    def own_rows(half, copies):
        received(copies)
        quad = pl.ds(4 * half, 4)
        kall[c, quad, x, spot, :] = in_order(rsz.at[half])
        return kall.at[c, quad, x, spot, :]

    def along_x(half, copies):
        return same(own_rows(half, copies), p1_s.at[0], p1_r.at[0], peers_x)

    def along_u(half, copies):
        received(copies)
        return [
            same(kall.at[c, pl.ds(2 * d, 2), :, spot, :], p3_s.at[d], p3_r.at[d], peers_y)
            for d in (2 * half, 2 * half + 1)
        ]

    def own_along_u(copies):
        return same(own_rows(1, copies), p3_s.at[2], p3_r.at[2], peers_y)

    def whole_along_x(copies):
        received(copies)
        return [same(kall.at[c, pl.ds(2 * d, 2), x], p1_s.at[d - 1], p1_r.at[d - 1], peers_x) for d in (2, 3)]

    def swap(d, copies):
        received(copies)
        pair = pl.ds(2 * d, 2)
        over = send(kall.at[c, pair], kall.at[c, pair], p4_s.at[d], p4_r.at[d], partner)
        pending.append(over)
        return over

    whole.wait_recv()
    chip0.wait_recv()
    chip2.wait_recv()
    cross_gram(1)
    cross_gram(2)
    near = scatter(0)
    received(leaf_u)
    leaf_x = same(leaves.at[c, :, x], b1_s, b1_r, peers_x)
    hop3 = hop(3, x, first, to_left, x_ref.at[first])
    hop4.wait_recv()
    chip4 = passed(4, across, first)
    hop5.wait_recv()
    chip5 = passed(5, across, last)
    near = spread(0, near)
    chip4.wait_recv()
    chip5.wait_recv()
    cross_gram(3)
    cross_gram(4)
    far = scatter(1)
    received(leaf_x)
    over = send(leaves.at[c], leaves.at[c], b4_s, b4_r, partner)
    pending.append(over)
    near = along_x(0, near)
    far = spread(1, far)
    over.wait_recv()

    def leaf(o):
        gx, gc = at(o)
        return jnp.concatenate([leaves[gc, 0, gx], leaves[gc, 1, gx]], 0)

    def leaf_roots(first_o):
        some, images = inverse_roots([leaf(first_o + i) for i in range(4)])
        for i in range(4):
            roots[first_o + i] = some[i]
            roots[8 + first_o + i] = images[i]

    leaf_roots(0)
    near = along_u(0, near)
    leaf_roots(4)
    far = own_along_u(far)
    hop3.wait_recv()
    chip3 = passed(3, right, first)
    chip1.wait_recv()
    chip3.wait_recv()
    for o in (5, 6, 7):
        prepare(o)
    overs = [swap(0, near[0])]
    far = whole_along_x(far)

    def gate(d):
        if d == 2:
            overs.append(swap(3, far[1]))
        overs[d].wait_recv()
        if d == 0:
            overs.append(swap(1, near[1]))
        if d == 1:
            overs.append(swap(2, far[0]))

    def stored(o, d):
        gx, gc = at(o)
        return jnp.concatenate([kall[gc, 2 * d - 2, gx], kall[gc, 2 * d - 1, gx]], 0)

    def block(a, b):
        return stored(a, b - a) if b - a <= 4 else stored(b, 8 - b + a).T

    def halves():
        return [jnp.concatenate([ref[o] for o in range(7, -1, -1)], 1) for ref in (xh, xl)]

    coef_ref[...], def_ref[...] = tree(
        lambda o: roots[o],
        lambda o: roots[8 + o],
        block,
        leaf(0),
        lambda level: sk_ref[level],
        halves,
        gate,
    )
    for copy in pending:
        copy.wait_send()


def outputs(x_ref, removed_ref, turned_ref, coefficients_ref, deflated_ref):
    coefficients_ref[...] = turned_ref[...].T
    deflated_ref[...] = x_ref[...] - removed_ref[...]


def body(snapshots, sketches):
    dma = pltpu.SemaphoreType.DMA
    vmem = pl.BlockSpec(memory_space=pltpu.VMEM)
    counts = [6, 6, 7, 7, (2, 7), (2, 7), (2, 7), (2, 7), (3, 3), (3, 3), (3, 7), (3, 7), 4, 4, 7, 7, 7, 7, 3, 3, 7, 7]
    shapes = [
        (NC, NZ, NX, 64, N),
        (NC, 2, NX, 64, N),
        (16, N, N),
        (4, 2, 64, N),
        (2, NY - 1, 2, 2, 8, N),
        (2, NZ, 4, 8, N),
        (2, 64, N),
        (NY - 1, 2, 8, N),
        (NZ, 2, 8, N),
    ]
    turned, removed = pl.pallas_call(
        step,
        out_shape=[jax.ShapeDtypeStruct((N, N), F32), jax.ShapeDtypeStruct((ROWS, N), F32)],
        in_specs=[pl.BlockSpec(memory_space=pl.ANY), vmem],
        out_specs=[vmem] * 2,
        scratch_shapes=[
            pltpu.VMEM((ROWS, N), F32),
            pltpu.VMEM((NX, NC, ROWS, N), F32),
            pltpu.VMEM((2 * NX, ROWS, N), BF),
            pltpu.VMEM((2 * NX, ROWS, N), BF),
            *[pltpu.VMEM(s, F32) for s in shapes],
            *[dma(n if isinstance(n, tuple) else (n,)) for n in counts],
            dma,
            dma,
            dma,
        ],
        compiler_params=pltpu.CompilerParams(collective_id=0, has_side_effects=True, vmem_limit_bytes=60 << 20),
        name="step",
    )(snapshots, sketches)
    return pl.pallas_call(
        outputs,
        out_shape=[jax.ShapeDtypeStruct((N, N), F32), jax.ShapeDtypeStruct((ROWS, N), F32)],
        in_specs=[vmem] * 3,
        out_specs=[vmem] * 2,
        name="outputs",
    )(snapshots, removed, turned)


def solution(mesh):
    placed = (P("row", "tm"), P())
    return jax.shard_map(
        body, mesh=mesh, in_specs=placed, out_specs=(P(None, "tm"), P("row", "tm")), check_vma=False
    )
```

```python
import jax
import jax.numpy as jnp
from jax import lax
from jax.experimental import pallas as pl
from jax.experimental.pallas import tpu as pltpu
from jax.sharding import PartitionSpec as P

BF, F32 = jnp.bfloat16, jnp.float32
MESH = pl.DeviceIdType.MESH
NX, NC, NY, NZ = 4, 2, 8, 8
N = 128
ROWS = 1024
SPLIT = 384


def split(a):
    high = a.astype(BF)
    return high, (a - high.astype(F32)).astype(BF)


def mm(a, b):
    ah, al = split(a)
    bh, bl = split(b)
    left = jnp.concatenate([ah, ah, al], 1)
    right = jnp.concatenate([bh, bl, bh], 0)
    return jnp.dot(left, right, preferred_element_type=F32)


def identity():
    down = lax.broadcasted_iota(jnp.int32, (N, N), 0)
    across = lax.broadcasted_iota(jnp.int32, (N, N), 1)
    return jnp.where(down == across, 1.0, 0.0).astype(F32)


def inverse_roots(grams, want_image=True, midway=None):
    one = identity()
    scales = [jnp.sqrt(jnp.sum(a * a, keepdims=True) + 1e-06) for a in grams]
    ts = [a / s for a, s in zip(grams, scales)]
    zs = ms = [1.5 * one - 0.5 * t for t in ts]
    ts = [mm(mm(t, m), m) for t, m in zip(ts, ms)]
    for step in range(1, 5):
        if step == 3 and midway is not None:
            midway()
        ms = [1.5 * one - 0.5 * t for t in ts]
        if step == 4 and not want_image:
            zs = [mm(z, m) for z, m in zip(zs, ms)]
        else:
            both = [mm(m, jnp.concatenate([t, z], 1)) for t, z, m in zip(ts, zs, ms)]
            zs = [b[:, N:] for b in both]
            ts = [mm(b[:, :N], m) for b, m in zip(both, ms)]
    return [z / jnp.sqrt(s) for z, s in zip(zs, scales)], ts


def sketched(t_p, t_g, cross, sketch):
    top = jnp.concatenate([t_p, cross.T], 1)
    bottom = jnp.concatenate([cross, t_g], 1)
    gram = jnp.concatenate([top, bottom], 0)
    s_t = mm(sketch.T, gram)
    s = s_t.T
    return s, mm(mm(s_t, gram), s)


def tree(root, image, block, own, sketch, halves, gate):
    gate(0)
    r = [root(o) for o in range(8)]
    s0, a0, e0 = [], [], []
    for j in range(4):
        cross = mm(mm(r[2 * j], block(2 * j, 2 * j + 1)), r[2 * j + 1])
        s, a = sketched(image(2 * j + 1), image(2 * j), cross, sketch(0))
        s0.append(s)
        a0.append(a)
    for j in range(4):
        e0.append(jnp.concatenate([mm(r[2 * j + 1], s0[j][:N]), mm(r[2 * j], s0[j][N:])], 0))
    r1, t1 = inverse_roots(a0, midway=lambda: gate(1))
    gate(2)
    cross1 = []
    for j in range(0, 4, 2):
        upper = jnp.concatenate([block(2 * j + 1, 2 * j + 3), block(2 * j + 1, 2 * j + 2)], 1)
        lower = jnp.concatenate([block(2 * j, 2 * j + 3), block(2 * j, 2 * j + 2)], 1)
        cross1.append(mm(e0[j].T, mm(jnp.concatenate([upper, lower], 0), e0[j + 1])))
    s1, a1, e1 = [], [], []
    for j in range(2):
        cross = mm(mm(r1[2 * j], cross1[j]), r1[2 * j + 1])
        s, a = sketched(t1[2 * j + 1], t1[2 * j], cross, sketch(1))
        s1.append(s)
        a1.append(a)
    for j in range(2):
        upper = mm(e0[2 * j + 1], mm(r1[2 * j + 1], s1[j][:N]))
        lower = mm(e0[2 * j], mm(r1[2 * j], s1[j][N:]))
        e1.append(jnp.concatenate([upper, lower], 0))
    r2, t2 = inverse_roots(a1)
    gate(3)
    wide = [jnp.concatenate([block(a, b) for b in (7, 6, 5, 4)], 1) for a in (3, 2, 1, 0)]
    cross2 = mm(e1[0].T, mm(jnp.concatenate(wide, 0), e1[1]))
    near = jnp.concatenate([block(0, 3), block(0, 2), block(0, 1), own], 1)
    far = jnp.concatenate([block(0, 7), block(0, 6), block(0, 5), block(0, 4)], 1)
    w_far, w_near = mm(far, e1[1]), mm(near, e1[0])
    s2, a2 = sketched(t2[1], t2[0], mm(mm(r2[0], cross2), r2[1]), sketch(2))
    h = mm(jnp.concatenate([mm(w_far, r2[1]), mm(w_near, r2[0])], 1), s2)
    upper = mm(e1[1], mm(r2[1], s2[:N]))
    lower = mm(e1[0], mm(r2[0], s2[N:]))
    high, low = halves()
    mix_h, mix_l = split(jnp.concatenate([upper, lower], 0))
    wide = jnp.concatenate([high, high, low], 1)
    base = jnp.dot(wide, jnp.concatenate([mix_h, mix_l, mix_h], 0), preferred_element_type=F32)
    r3 = inverse_roots([a2], False)[0][0]
    turned = mm(h, r3)
    return turned, mm(base, mm(r3, turned.T))


def place():
    tm, row = lax.axis_index("tm"), lax.axis_index("row")
    c = tm % NC
    y, z = row % NY, row // NY
    return tm // NC, c, y + c * (z - y), z + c * (y - z)


def device(x, c, core, u, v):
    y, z = u + core * (v - u), v + core * (u - v)
    return (x * NC + c, z * NY + y)


def rows_of(index, count):
    return pl.ds(pl.multiple_of(index * count, count), count)


def step(x_hbm, sk_ref, coef_ref, def_ref, x_ref, xall, xh, xl, kall, leaves, roots, part, rsy, rsz, lrow, lsy, lsz,
         g_s, g_r, c_s, c_r, y_s, y_r, z_s, z_r, p1_s, p1_r, p3_s, p3_r, p4_s, p4_r,
         ly_s, ly_r, lz_s, lz_r, b1_s, b1_r, b2_s, b2_r, b4_s, b4_r, load_s):
    x, c, u, v = place()
    tm = x * NC + c
    left, right, across = (x + 3) % NX, (x + 1) % NX, (x + 2) % NX
    peers_x = [device((x + k) % NX, c, c, u, v) for k in range(1, NX)]
    peers_y = [device(x, c, c, (u + k) % NY, v) for k in range(1, NY)]
    peers_z = [device(x, c, c, u, (v + k) % NZ) for k in range(1, NZ)]
    partner = device(x, 1 - c, c, u, v)

    barrier = pltpu.get_barrier_semaphore()
    everyone = peers_x + peers_y + peers_z + [partner]
    for peer in everyone:
        pl.semaphore_signal(barrier, inc=1, device_id=peer, device_id_type=MESH)
    load = pltpu.make_async_copy(x_hbm, x_ref, load_s)
    load.start()
    load.wait()

    mine = x_ref[...]
    xall[x, c] = mine
    mine_h, mine_l = split(mine)
    xh[0] = mine_h
    xl[0] = mine_l
    turned_h, turned_l = split(mine.T)
    turned = jnp.concatenate([turned_h, turned_h, turned_l], 1)

    def gram_with(high, low):
        return jnp.dot(turned, jnp.concatenate([high, low, high], 0), preferred_element_type=F32)

    lrow[...] = gram_with(mine_h, mine_l).reshape(2, 64, N)
    pl.semaphore_wait(barrier, len(everyone))

    def send(src, dst, s, r, peer):
        copy = pltpu.make_async_remote_copy(
            src_ref=src, dst_ref=dst, send_sem=s, recv_sem=r, device_id=peer, device_id_type=MESH
        )
        copy.start()
        return copy

    pending = []
    first, last = pl.ds(0, SPLIT), pl.ds(SPLIT, ROWS - SPLIT)
    to_right, to_left = device(right, c, c, u, v), device(left, c, c, u, v)

    def hop(k, source, part_of, peer, src=None):
        src = xall.at[source, c, part_of] if src is None else src
        copy = send(src, xall.at[source, c, part_of], g_s.at[k], g_r.at[k], peer)
        pending.append(copy)
        return copy

    def passed(k, source, part_of):
        here = xall.at[source, c, part_of]
        copy = send(here, here, c_s.at[k], c_r.at[k], partner)
        pending.append(copy)
        return copy

    hop0 = hop(0, x, first, to_right, x_ref.at[first])
    hop1 = hop(1, x, last, to_left, x_ref.at[last])
    hop2 = hop(2, x, last, to_right, x_ref.at[last])
    whole = send(x_ref, xall.at[x, c], c_s.at[6], c_r.at[6], partner)
    pending.append(whole)
    copies = [
        send(lrow.at[:, rows_of((u + k) % NY, 8), :], lsy.at[k - 1], ly_s.at[k - 1], ly_r.at[k - 1], peers_y[k - 1])
        for k in range(1, NY)
    ]
    total = lrow[:, rows_of(u, 8), :]
    for k, copy in enumerate(copies):
        copy.wait_recv()
        total += lsy[k]
    pending += copies
    lsz[NZ - 1] = total
    copies = [
        send(lsz.at[NZ - 1], lsz.at[k - 1], lz_s.at[k - 1], lz_r.at[k - 1], peers_z[k - 1])
        for k in range(1, NZ)
    ]

    hop0.wait_recv()
    hop4 = hop(4, left, first, to_right)
    chip0 = passed(0, left, first)

    def in_order(slots):
        total = slots[(v + NZ - 1) % NZ]
        for source in range(1, NZ):
            total += slots[(v - source + NZ - 1) % NZ]
        return total

    def received(copies):
        for copy in copies:
            copy.wait_recv()
        pending.extend(copies)

    spot = rows_of(u, 8)

    def at(o):
        g = (tm - o + 8) % 8
        return g // NC, g % NC

    def to_line(src, dst, s, r, peers):
        return [send(src, dst, s.at[k], r.at[k], peer) for k, peer in enumerate(peers)]

    def same(ref, s, r, peers):
        return to_line(ref, ref, s, r, peers)

    received(copies)
    leaves[c, :, x, spot, :] = in_order(lsz)
    leaf_u = same(leaves.at[c, :, x, spot, :], b2_s, b2_r, peers_y)
    hop1.wait_recv()
    hop5 = hop(5, right, last, to_left)
    chip1 = passed(1, right, last)
    hop2.wait_recv()
    chip2 = passed(2, left, last)

    def prepare(o):
        gx, gc = at(o)
        high, low = split(xall[gx, gc])
        xh[o] = high
        xl[o] = low
        return high, low

    def cross_gram(d):
        part[d - 1] = gram_with(*prepare(d)).reshape(2, 64, N)

    def scatter(half):
        pair = pl.ds(2 * half, 2)
        return [
            send(
                part.at[pair, :, rows_of((u + k) % NY, 8), :],
                rsy.at[half, k - 1],
                y_s.at[half, k - 1],
                y_r.at[half, k - 1],
                peers_y[k - 1],
            )
            for k in range(1, NY)
        ]

    def spread(half, copies):
        received(copies)
        total = part[2 * half : 2 * half + 2, :, spot, :]
        for k in range(NY - 1):
            total += rsy[half, k]
        rsz[half, NZ - 1] = total.reshape(4, 8, N)
        return [
            send(rsz.at[half, NZ - 1], rsz.at[half, k], z_s.at[half, k], z_r.at[half, k], peers_z[k])
            for k in range(NZ - 1)
        ]

    def own_rows(half, copies):
        received(copies)
        quad = pl.ds(4 * half, 4)
        kall[c, quad, x, spot, :] = in_order(rsz.at[half])
        return kall.at[c, quad, x, spot, :]

    def along_x(half, copies):
        return same(own_rows(half, copies), p1_s.at[0], p1_r.at[0], peers_x)

    def along_u(half, copies):
        received(copies)
        return [
            same(kall.at[c, pl.ds(2 * d, 2), :, spot, :], p3_s.at[d], p3_r.at[d], peers_y)
            for d in (2 * half, 2 * half + 1)
        ]

    def far_first(copies):
        own_rows(1, copies)
        by_x = same(kall.at[c, pl.ds(4, 2), x, spot, :], p1_s.at[1], p1_r.at[1], peers_x)
        return by_x, same(kall.at[c, pl.ds(6, 2), x, spot, :], p3_s.at[3], p3_r.at[3], peers_y)

    def far_last(by_x, by_u):
        received(by_x)
        by_x = same(kall.at[c, pl.ds(4, 2), :, spot, :], p3_s.at[2], p3_r.at[2], peers_y)
        received(by_u)
        return by_x, same(kall.at[c, pl.ds(6, 2), x], p1_s.at[2], p1_r.at[2], peers_x)

    def swap(d, copies):
        received(copies)
        pair = pl.ds(2 * d, 2)
        over = send(kall.at[c, pair], kall.at[c, pair], p4_s.at[d], p4_r.at[d], partner)
        pending.append(over)
        return over

    whole.wait_recv()
    chip0.wait_recv()
    chip2.wait_recv()
    cross_gram(1)
    cross_gram(2)
    near = scatter(0)
    received(leaf_u)
    leaf_x = same(leaves.at[c, :, x], b1_s, b1_r, peers_x)
    hop3 = hop(3, x, first, to_left, x_ref.at[first])
    hop4.wait_recv()
    chip4 = passed(4, across, first)
    hop5.wait_recv()
    chip5 = passed(5, across, last)
    near = spread(0, near)
    chip4.wait_recv()
    chip5.wait_recv()
    cross_gram(3)
    cross_gram(4)
    far = scatter(1)
    received(leaf_x)
    over = send(leaves.at[c], leaves.at[c], b4_s, b4_r, partner)
    pending.append(over)
    near = along_x(0, near)
    far = spread(1, far)
    over.wait_recv()

    def leaf(o):
        gx, gc = at(o)
        return jnp.concatenate([leaves[gc, 0, gx], leaves[gc, 1, gx]], 0)

    def leaf_roots(first_o):
        some, images = inverse_roots([leaf(first_o + i) for i in range(4)])
        for i in range(4):
            roots[first_o + i] = some[i]
            roots[8 + first_o + i] = images[i]

    leaf_roots(0)
    near = along_u(0, near)
    leaf_roots(4)
    far = far_first(far)
    hop3.wait_recv()
    chip3 = passed(3, right, first)
    chip1.wait_recv()
    far = far_last(*far)
    chip3.wait_recv()
    for o in (5, 6, 7):
        prepare(o)
    overs = [swap(0, near[0])]

    def gate(d):
        if d == 2:
            overs.append(swap(3, far[1]))
        overs[d].wait_recv()
        if d == 0:
            overs.append(swap(1, near[1]))
        if d == 1:
            overs.append(swap(2, far[0]))

    def stored(o, d):
        gx, gc = at(o)
        return jnp.concatenate([kall[gc, 2 * d - 2, gx], kall[gc, 2 * d - 1, gx]], 0)

    def block(a, b):
        return stored(a, b - a) if b - a <= 4 else stored(b, 8 - b + a).T

    def halves():
        return [jnp.concatenate([ref[o] for o in range(7, -1, -1)], 1) for ref in (xh, xl)]

    coef_ref[...], def_ref[...] = tree(
        lambda o: roots[o],
        lambda o: roots[8 + o],
        block,
        leaf(0),
        lambda level: sk_ref[level],
        halves,
        gate,
    )
    for copy in pending:
        copy.wait_send()


def outputs(x_ref, removed_ref, turned_ref, coefficients_ref, deflated_ref):
    coefficients_ref[...] = turned_ref[...].T
    deflated_ref[...] = x_ref[...] - removed_ref[...]


def body(snapshots, sketches):
    dma = pltpu.SemaphoreType.DMA
    vmem = pl.BlockSpec(memory_space=pltpu.VMEM)
    counts = [6, 6, 7, 7, (2, 7), (2, 7), (2, 7), (2, 7), (3, 3), (3, 3), (4, 7), (4, 7), 4, 4, 7, 7, 7, 7, 3, 3, 7, 7]
    shapes = [
        (NC, NZ, NX, 64, N),
        (NC, 2, NX, 64, N),
        (16, N, N),
        (4, 2, 64, N),
        (2, NY - 1, 2, 2, 8, N),
        (2, NZ, 4, 8, N),
        (2, 64, N),
        (NY - 1, 2, 8, N),
        (NZ, 2, 8, N),
    ]
    turned, removed = pl.pallas_call(
        step,
        out_shape=[jax.ShapeDtypeStruct((N, N), F32), jax.ShapeDtypeStruct((ROWS, N), F32)],
        in_specs=[pl.BlockSpec(memory_space=pl.ANY), vmem],
        out_specs=[vmem] * 2,
        scratch_shapes=[
            pltpu.VMEM((ROWS, N), F32),
            pltpu.VMEM((NX, NC, ROWS, N), F32),
            pltpu.VMEM((2 * NX, ROWS, N), BF),
            pltpu.VMEM((2 * NX, ROWS, N), BF),
            *[pltpu.VMEM(s, F32) for s in shapes],
            *[dma(n if isinstance(n, tuple) else (n,)) for n in counts],
            dma,
            dma,
            dma,
        ],
        compiler_params=pltpu.CompilerParams(collective_id=0, has_side_effects=True, vmem_limit_bytes=60 << 20),
        name="step",
    )(snapshots, sketches)
    return pl.pallas_call(
        outputs,
        out_shape=[jax.ShapeDtypeStruct((N, N), F32), jax.ShapeDtypeStruct((ROWS, N), F32)],
        in_specs=[vmem] * 3,
        out_specs=[vmem] * 2,
        name="outputs",
    )(snapshots, removed, turned)


def solution(mesh):
    placed = (P("row", "tm"), P())
    return jax.shard_map(
        body, mesh=mesh, in_specs=placed, out_specs=(P(None, "tm"), P("row", "tm")), check_vma=False
    )
```

```python
import jax
import jax.numpy as jnp
from jax import lax
from jax.experimental import pallas as pl
from jax.experimental.pallas import tpu as pltpu
from jax.sharding import PartitionSpec as P

BF, F32 = jnp.bfloat16, jnp.float32
MESH = pl.DeviceIdType.MESH
NX, NC, NY, NZ = 4, 2, 8, 8
N = 128
ROWS = 1024
SPLIT = 384


def split(a):
    high = a.astype(BF)
    return high, (a - high.astype(F32)).astype(BF)


def mm(a, b):
    ah, al = split(a)
    bh, bl = split(b)
    left = jnp.concatenate([ah, ah, al], 1)
    right = jnp.concatenate([bh, bl, bh], 0)
    return jnp.dot(left, right, preferred_element_type=F32)


def identity():
    down = lax.broadcasted_iota(jnp.int32, (N, N), 0)
    across = lax.broadcasted_iota(jnp.int32, (N, N), 1)
    return jnp.where(down == across, 1.0, 0.0).astype(F32)


def inverse_roots(grams, want_image=True, midway=None):
    one = identity()
    scales = [jnp.sqrt(jnp.sum(a * a, keepdims=True) + 1e-06) for a in grams]
    ts = [a / s for a, s in zip(grams, scales)]
    zs = ms = [1.5 * one - 0.5 * t for t in ts]
    ts = [mm(mm(t, m), m) for t, m in zip(ts, ms)]
    for step in range(1, 5):
        if step == 3 and midway is not None:
            midway()
        ms = [1.5 * one - 0.5 * t for t in ts]
        if step == 4 and not want_image:
            zs = [mm(z, m) for z, m in zip(zs, ms)]
        else:
            both = [mm(m, jnp.concatenate([t, z], 1)) for t, z, m in zip(ts, zs, ms)]
            zs = [b[:, N:] for b in both]
            ts = [mm(b[:, :N], m) for b, m in zip(both, ms)]
    return [z / jnp.sqrt(s) for z, s in zip(zs, scales)], ts


def sketched(t_p, t_g, cross, sketch):
    top = jnp.concatenate([t_p, cross.T], 1)
    bottom = jnp.concatenate([cross, t_g], 1)
    gram = jnp.concatenate([top, bottom], 0)
    s_t = mm(sketch.T, gram)
    s = s_t.T
    return s, mm(mm(s_t, gram), s)


def tree(root, image, block, own, sketch, halves, gate):
    gate(0)
    r = [root(o) for o in range(8)]
    s0, a0, e0 = [], [], []
    for j in range(4):
        cross = mm(mm(r[2 * j], block(2 * j, 2 * j + 1)), r[2 * j + 1])
        s, a = sketched(image(2 * j + 1), image(2 * j), cross, sketch(0))
        s0.append(s)
        a0.append(a)
    for j in range(4):
        e0.append(jnp.concatenate([mm(r[2 * j + 1], s0[j][:N]), mm(r[2 * j], s0[j][N:])], 0))
    r1, t1 = inverse_roots(a0, midway=lambda: gate(1))
    gate(2)
    cross1 = []
    for j in range(0, 4, 2):
        upper = jnp.concatenate([block(2 * j + 1, 2 * j + 3), block(2 * j + 1, 2 * j + 2)], 1)
        lower = jnp.concatenate([block(2 * j, 2 * j + 3), block(2 * j, 2 * j + 2)], 1)
        cross1.append(mm(e0[j].T, mm(jnp.concatenate([upper, lower], 0), e0[j + 1])))
    s1, a1, e1 = [], [], []
    for j in range(2):
        cross = mm(mm(r1[2 * j], cross1[j]), r1[2 * j + 1])
        s, a = sketched(t1[2 * j + 1], t1[2 * j], cross, sketch(1))
        s1.append(s)
        a1.append(a)
    for j in range(2):
        upper = mm(e0[2 * j + 1], mm(r1[2 * j + 1], s1[j][:N]))
        lower = mm(e0[2 * j], mm(r1[2 * j], s1[j][N:]))
        e1.append(jnp.concatenate([upper, lower], 0))
    r2, t2 = inverse_roots(a1)
    gate(3)
    wide = [jnp.concatenate([block(a, b) for b in (7, 6, 5, 4)], 1) for a in (3, 2, 1, 0)]
    cross2 = mm(e1[0].T, mm(jnp.concatenate(wide, 0), e1[1]))
    near = jnp.concatenate([block(0, 3), block(0, 2), block(0, 1), own], 1)
    far = jnp.concatenate([block(0, 7), block(0, 6), block(0, 5), block(0, 4)], 1)
    w_far, w_near = mm(far, e1[1]), mm(near, e1[0])
    s2, a2 = sketched(t2[1], t2[0], mm(mm(r2[0], cross2), r2[1]), sketch(2))
    h = mm(jnp.concatenate([mm(w_far, r2[1]), mm(w_near, r2[0])], 1), s2)
    upper = mm(e1[1], mm(r2[1], s2[:N]))
    lower = mm(e1[0], mm(r2[0], s2[N:]))
    high, low = halves()
    mix_h, mix_l = split(jnp.concatenate([upper, lower], 0))
    wide = jnp.concatenate([high, high, low], 1)
    base = jnp.dot(wide, jnp.concatenate([mix_h, mix_l, mix_h], 0), preferred_element_type=F32)
    r3 = inverse_roots([a2], False)[0][0]
    turned = mm(h, r3)
    return turned, mm(base, mm(r3, turned.T))


def place():
    tm, row = lax.axis_index("tm"), lax.axis_index("row")
    c = tm % NC
    y, z = row % NY, row // NY
    return tm // NC, c, y + c * (z - y), z + c * (y - z)


def device(x, c, core, u, v):
    y, z = u + core * (v - u), v + core * (u - v)
    return (x * NC + c, z * NY + y)


def rows_of(index, count):
    return pl.ds(pl.multiple_of(index * count, count), count)


def step(x_hbm, sk_ref, coef_ref, def_ref, x_ref, xall, xh, xl, kall, leaves, roots, part, rsy, rsz, lrow, lsy, lsz,
         g_s, g_r, c_s, c_r, y_s, y_r, z_s, z_r, p1_s, p1_r, p3_s, p3_r, p4_s, p4_r,
         ly_s, ly_r, lz_s, lz_r, b1_s, b1_r, b2_s, b2_r, b4_s, b4_r, load_s):
    x, c, u, v = place()
    tm = x * NC + c
    left, right, across = (x + 3) % NX, (x + 1) % NX, (x + 2) % NX
    peers_x = [device((x + k) % NX, c, c, u, v) for k in range(1, NX)]
    peers_y = [device(x, c, c, (u + k) % NY, v) for k in range(1, NY)]
    peers_z = [device(x, c, c, u, (v + k) % NZ) for k in range(1, NZ)]
    partner = device(x, 1 - c, c, u, v)

    barrier = pltpu.get_barrier_semaphore()
    everyone = peers_x + peers_y + peers_z + [partner]
    for peer in everyone:
        pl.semaphore_signal(barrier, inc=1, device_id=peer, device_id_type=MESH)
    load = pltpu.make_async_copy(x_hbm, x_ref, load_s)
    load.start()
    load.wait()

    mine = x_ref[...]
    xall[x, c] = mine
    mine_h, mine_l = split(mine)
    xh[0] = mine_h
    xl[0] = mine_l
    turned_h, turned_l = split(mine.T)
    turned = jnp.concatenate([turned_h, turned_h, turned_l], 1)

    def gram_with(high, low):
        return jnp.dot(turned, jnp.concatenate([high, low, high], 0), preferred_element_type=F32)

    lrow[...] = gram_with(mine_h, mine_l).reshape(2, 64, N)
    pl.semaphore_wait(barrier, len(everyone))

    def send(src, dst, s, r, peer):
        copy = pltpu.make_async_remote_copy(
            src_ref=src, dst_ref=dst, send_sem=s, recv_sem=r, device_id=peer, device_id_type=MESH
        )
        copy.start()
        return copy

    pending = []
    first, last = pl.ds(0, SPLIT), pl.ds(SPLIT, ROWS - SPLIT)
    to_right, to_left = device(right, c, c, u, v), device(left, c, c, u, v)

    def hop(k, source, part_of, peer, src=None):
        src = xall.at[source, c, part_of] if src is None else src
        copy = send(src, xall.at[source, c, part_of], g_s.at[k], g_r.at[k], peer)
        pending.append(copy)
        return copy

    def passed(k, source, part_of):
        here = xall.at[source, c, part_of]
        copy = send(here, here, c_s.at[k], c_r.at[k], partner)
        pending.append(copy)
        return copy

    hop0 = hop(0, x, first, to_right, x_ref.at[first])
    hop1 = hop(1, x, last, to_left, x_ref.at[last])
    hop2 = hop(2, x, last, to_right, x_ref.at[last])
    whole = send(x_ref, xall.at[x, c], c_s.at[6], c_r.at[6], partner)
    pending.append(whole)
    copies = [
        send(lrow.at[:, rows_of((u + k) % NY, 8), :], lsy.at[k - 1], ly_s.at[k - 1], ly_r.at[k - 1], peers_y[k - 1])
        for k in range(1, NY)
    ]
    total = lrow[:, rows_of(u, 8), :]
    for k, copy in enumerate(copies):
        copy.wait_recv()
        total += lsy[k]
    pending += copies
    lsz[NZ - 1] = total
    copies = [
        send(lsz.at[NZ - 1], lsz.at[k - 1], lz_s.at[k - 1], lz_r.at[k - 1], peers_z[k - 1])
        for k in range(1, NZ)
    ]

    hop0.wait_recv()
    hop4 = hop(4, left, first, to_right)
    chip0 = passed(0, left, first)

    def in_order(slots):
        total = slots[(v + NZ - 1) % NZ]
        for source in range(1, NZ):
            total += slots[(v - source + NZ - 1) % NZ]
        return total

    def received(copies):
        for copy in copies:
            copy.wait_recv()
        pending.extend(copies)

    spot = rows_of(u, 8)

    def at(o):
        g = (tm - o + 8) % 8
        return g // NC, g % NC

    def to_line(src, dst, s, r, peers):
        return [send(src, dst, s.at[k], r.at[k], peer) for k, peer in enumerate(peers)]

    def same(ref, s, r, peers):
        return to_line(ref, ref, s, r, peers)

    received(copies)
    leaves[c, :, x, spot, :] = in_order(lsz)
    leaf_u = same(leaves.at[c, :, x, spot, :], b2_s, b2_r, peers_y)
    hop1.wait_recv()
    hop5 = hop(5, right, last, to_left)
    chip1 = passed(1, right, last)
    hop2.wait_recv()
    chip2 = passed(2, left, last)

    def prepare(o):
        gx, gc = at(o)
        high, low = split(xall[gx, gc])
        xh[o] = high
        xl[o] = low
        return high, low

    def cross_gram(d):
        part[d - 1] = gram_with(*prepare(d)).reshape(2, 64, N)

    def scatter(half):
        pair = pl.ds(2 * half, 2)
        return [
            send(
                part.at[pair, :, rows_of((u + k) % NY, 8), :],
                rsy.at[half, k - 1],
                y_s.at[half, k - 1],
                y_r.at[half, k - 1],
                peers_y[k - 1],
            )
            for k in range(1, NY)
        ]

    def spread(half, copies):
        received(copies)
        total = part[2 * half : 2 * half + 2, :, spot, :]
        for k in range(NY - 1):
            total += rsy[half, k]
        rsz[half, NZ - 1] = total.reshape(4, 8, N)
        return [
            send(rsz.at[half, NZ - 1], rsz.at[half, k], z_s.at[half, k], z_r.at[half, k], peers_z[k])
            for k in range(NZ - 1)
        ]

    def own_rows(half, copies):
        received(copies)
        quad = pl.ds(4 * half, 4)
        kall[c, quad, x, spot, :] = in_order(rsz.at[half])
        return kall.at[c, quad, x, spot, :]

    def along_x(half, copies):
        return same(own_rows(half, copies), p1_s.at[0], p1_r.at[0], peers_x)

    def along_u(half, copies):
        received(copies)
        return [
            same(kall.at[c, pl.ds(2 * d, 2), :, spot, :], p3_s.at[d], p3_r.at[d], peers_y)
            for d in (2 * half, 2 * half + 1)
        ]

    def far_first(copies):
        own_rows(1, copies)
        by_x = same(kall.at[c, pl.ds(4, 2), x, spot, :], p1_s.at[1], p1_r.at[1], peers_x)
        return by_x, same(kall.at[c, pl.ds(6, 2), x, spot, :], p3_s.at[3], p3_r.at[3], peers_y)

    def third_along_u(copies):
        received(copies)
        return same(kall.at[c, pl.ds(4, 2), :, spot, :], p3_s.at[2], p3_r.at[2], peers_y)

    def fourth_along_x(copies):
        received(copies)
        return same(kall.at[c, pl.ds(6, 2), x], p1_s.at[2], p1_r.at[2], peers_x)

    def swap(d, copies):
        received(copies)
        pair = pl.ds(2 * d, 2)
        over = send(kall.at[c, pair], kall.at[c, pair], p4_s.at[d], p4_r.at[d], partner)
        pending.append(over)
        return over

    whole.wait_recv()
    chip0.wait_recv()
    chip2.wait_recv()
    cross_gram(1)
    cross_gram(2)
    near = scatter(0)
    received(leaf_u)
    leaf_x = same(leaves.at[c, :, x], b1_s, b1_r, peers_x)
    hop3 = hop(3, x, first, to_left, x_ref.at[first])
    hop4.wait_recv()
    chip4 = passed(4, across, first)
    hop5.wait_recv()
    chip5 = passed(5, across, last)
    near = spread(0, near)
    chip4.wait_recv()
    chip5.wait_recv()
    cross_gram(3)
    cross_gram(4)
    far = scatter(1)
    received(leaf_x)
    over = send(leaves.at[c], leaves.at[c], b4_s, b4_r, partner)
    pending.append(over)
    near = along_x(0, near)
    far = spread(1, far)
    over.wait_recv()

    def leaf(o):
        gx, gc = at(o)
        return jnp.concatenate([leaves[gc, 0, gx], leaves[gc, 1, gx]], 0)

    def leaf_roots(first_o):
        some, images = inverse_roots([leaf(first_o + i) for i in range(4)])
        for i in range(4):
            roots[first_o + i] = some[i]
            roots[8 + first_o + i] = images[i]

    leaf_roots(0)
    near = along_u(0, near)
    leaf_roots(4)
    third, fourth = far_first(far)
    hop3.wait_recv()
    chip3 = passed(3, right, first)
    chip1.wait_recv()
    chip3.wait_recv()
    for o in (5, 6, 7):
        prepare(o)
    third = third_along_u(third)
    overs = [swap(0, near[0])]
    fourth = fourth_along_x(fourth)

    def gate(d):
        if d == 2:
            overs.append(swap(3, fourth))
        overs[d].wait_recv()
        if d == 0:
            overs.append(swap(1, near[1]))
        if d == 1:
            overs.append(swap(2, third))

    def stored(o, d):
        gx, gc = at(o)
        return jnp.concatenate([kall[gc, 2 * d - 2, gx], kall[gc, 2 * d - 1, gx]], 0)

    def block(a, b):
        return stored(a, b - a) if b - a <= 4 else stored(b, 8 - b + a).T

    def halves():
        return [jnp.concatenate([ref[o] for o in range(7, -1, -1)], 1) for ref in (xh, xl)]

    coef_ref[...], def_ref[...] = tree(
        lambda o: roots[o],
        lambda o: roots[8 + o],
        block,
        leaf(0),
        lambda level: sk_ref[level],
        halves,
        gate,
    )
    for copy in pending:
        copy.wait_send()


def outputs(x_ref, removed_ref, turned_ref, coefficients_ref, deflated_ref):
    coefficients_ref[...] = turned_ref[...].T
    deflated_ref[...] = x_ref[...] - removed_ref[...]


def body(snapshots, sketches):
    dma = pltpu.SemaphoreType.DMA
    vmem = pl.BlockSpec(memory_space=pltpu.VMEM)
    counts = [6, 6, 7, 7, (2, 7), (2, 7), (2, 7), (2, 7), (3, 3), (3, 3), (4, 7), (4, 7), 4, 4, 7, 7, 7, 7, 3, 3, 7, 7]
    shapes = [
        (NC, NZ, NX, 64, N),
        (NC, 2, NX, 64, N),
        (16, N, N),
        (4, 2, 64, N),
        (2, NY - 1, 2, 2, 8, N),
        (2, NZ, 4, 8, N),
        (2, 64, N),
        (NY - 1, 2, 8, N),
        (NZ, 2, 8, N),
    ]
    turned, removed = pl.pallas_call(
        step,
        out_shape=[jax.ShapeDtypeStruct((N, N), F32), jax.ShapeDtypeStruct((ROWS, N), F32)],
        in_specs=[pl.BlockSpec(memory_space=pl.ANY), vmem],
        out_specs=[vmem] * 2,
        scratch_shapes=[
            pltpu.VMEM((ROWS, N), F32),
            pltpu.VMEM((NX, NC, ROWS, N), F32),
            pltpu.VMEM((2 * NX, ROWS, N), BF),
            pltpu.VMEM((2 * NX, ROWS, N), BF),
            *[pltpu.VMEM(s, F32) for s in shapes],
            *[dma(n if isinstance(n, tuple) else (n,)) for n in counts],
            dma,
            dma,
            dma,
        ],
        compiler_params=pltpu.CompilerParams(collective_id=0, has_side_effects=True, vmem_limit_bytes=60 << 20),
        name="step",
    )(snapshots, sketches)
    return pl.pallas_call(
        outputs,
        out_shape=[jax.ShapeDtypeStruct((N, N), F32), jax.ShapeDtypeStruct((ROWS, N), F32)],
        in_specs=[vmem] * 3,
        out_specs=[vmem] * 2,
        name="outputs",
    )(snapshots, removed, turned)


def solution(mesh):
    placed = (P("row", "tm"), P())
    return jax.shard_map(
        body, mesh=mesh, in_specs=placed, out_specs=(P(None, "tm"), P("row", "tm")), check_vma=False
    )
```
